32 devices in a mesh: dp: 4 (over z), mp: 8 (over y, x, core).
Axes of the slice: x: 2, y: 2, z: 4, core: 2. Of those that a mesh axis runs over, the one named last changes fastest.
Arguments:
- tokens: bfloat16 [16384, 2048], P('dp', 'mp'), may hold values from -6 to 6
- norm_gains: float32 [2, 2048], replicated, may hold values from 0.5 to 1.5
- query_key_value_weight: bfloat16 [3, 2048, 2048], P(None, None, 'mp'), may hold values from -0.125 to 0.125
- output_weight: bfloat16 [2048, 2048], P('mp'), may hold values from -0.125 to 0.125
- gate_up_weight: bfloat16 [2, 2048, 5632], P(None, None, 'mp'), may hold values from -0.125 to 0.125
- down_weight: bfloat16 [5632, 2048], P('mp'), may hold values from -0.078125 to 0.078125
- a_in: float32 [6, 2048, 16], P(None, ('dp', 'mp')), may hold values from -0.125 to 0.125
- a_down: float32 [5632, 16], P(('dp', 'mp')), may hold values from -0.078125 to 0.078125
- b_dmodel: float32 [5, 16, 2048], P(None, None, ('dp', 'mp')), may hold values from -0.375 to 0.375
- b_hidden: float32 [2, 16, 5632], P(None, None, ('dp', 'mp')), may hold values from -0.375 to 0.375
- m_dmodel: float32 [5, 2048], P(None, ('dp', 'mp')), may hold values from 0.8 to 8, as said below
- m_hidden: float32 [2, 5632], P(None, ('dp', 'mp')), may hold values from 0.7 to 1.6
- segment_ids: int32 [8, 2048], P('dp'), may hold values from 0 to 7, as said below
- valid_mask: int32 [8, 2048], P('dp'), may hold values from 0 to 1, as said below
- cotangent: bfloat16 [16384, 2048], P('dp', 'mp'), may hold values from -6 to 6
Outputs:
- activations: bfloat16 [16384, 2048], P('dp', 'mp')
- input_grad: bfloat16 [16384, 2048], P('dp', 'mp')
- grad_a_in: float32 [6, 2048, 16], P(None, ('dp', 'mp'))
- grad_a_down: float32 [5632, 16], P(('dp', 'mp'))
- grad_b_dmodel: float32 [5, 16, 2048], P(None, None, ('dp', 'mp'))
- grad_b_hidden: float32 [2, 16, 5632], P(None, None, ('dp', 'mp'))
- grad_m_dmodel: float32 [5, 2048], P(None, ('dp', 'mp'))
- grad_m_hidden: float32 [2, 5632], P(None, ('dp', 'mp'))
The draws below stay inside these ranges and needn't reach their ends.
Inputs may be any that keep to these rules, and one draw needn't show every extreme that they name: `segment_ids`: in each row the segment numbers never fall, begin at 0 and take every value up to 7. `valid_mask`: in each row the ones come first, followed by 1 to 256 zeros. `m_dmodel`: magnitudes of q, k and v lie in 0.8 to 1.6, of o in 3 to 8, of down in 1.2 to 3.
All inputs are finite; a program needn't handle non-finite values.
Results may differ from the reference program's by a relative error of at most 0.025.
Values may be sent and summed in bfloat16 or wider, within the bound.
No kernel may reach another device: no remote copies, remote signals or barrier semaphores. Data moves between devices by JAX's collectives and lax.ppermute only.
A program may use at most 384 MiB of HBM per device.

```python
import math
import jax
import jax.numpy as jnp
from jax import lax

D = 2048
H = 16
HEAD = 128
FF = 5632
RANK = 16
SEQ = 2048
NSEG = 8
ROWS_DEV = 2
ROWS = 8
TOKENS = 16384
N_DP = 4
N_MP = 8


def draw_m_dmodel(key, part):
    lower_end = jnp.array([0.8, 0.8, 0.8, 3.0, 1.2], jnp.float32)
    upper_end = jnp.array([1.6, 1.6, 1.6, 8.0, 3.0], jnp.float32)
    fraction = jax.random.uniform(key, (5, D), jnp.float32)
    return jnp.exp(jnp.log(lower_end)[:, None] + fraction * jnp.log(upper_end / lower_end)[:, None])


def draw_segment_ids(key, part):
    row_keys = jax.random.split(key, ROWS)

    def one_row(row_key):
        order = jax.random.permutation(row_key, SEQ - 1)
        cuts = jnp.sort(order[:NSEG - 1] + 1).astype(jnp.int32)
        index = jnp.arange(SEQ, dtype=jnp.int32)
        return jnp.sum((cuts[None, :] <= index[:, None]).astype(jnp.int32), axis=1)
    return jax.vmap(one_row)(row_keys).astype(jnp.int32)


def draw_valid_mask(key, part):
    padding = jax.random.randint(key, (ROWS, 1), 1, SEQ // 8 + 1)
    index = jnp.arange(SEQ, dtype=jnp.int32)[None, :]
    return (index < SEQ - padding).astype(jnp.int32)


def block_levels(rng, shape, cuts, smallest, top_value):
    factor_of = 1.0
    for axis_at, parts in cuts:
        steps = jax.random.uniform(jax.random.fold_in(jax.random.fold_in(rng, 6), axis_at), (parts,), jnp.float32, smallest / len(cuts), top_value / len(cuts))
        factor_of = factor_of * jnp.repeat(jnp.exp(steps), shape[axis_at] // parts).reshape((-1,) + (1,) * (len(shape) - 1 - axis_at))
    return factor_of


def gaussian(key, dims, width, reach, cuts=(), kind=jnp.bfloat16):
    values = width * jax.random.normal(key, dims, jnp.float32)
    if cuts:
        values = values * block_levels(key, dims, cuts, -0.22, 0.18)
    return jnp.clip(values, -reach, reach).astype(kind)


def setup_inputs(seed: int = 0) -> dict:
    key_list = jax.random.split(jax.random.key(seed), 16)
    return {
        "tokens": gaussian(key_list[0], (TOKENS, D), 1.0, 6.0, ((0, 4), (1, 8))),
        "norm_gains": jnp.clip(1.0 + 0.1 * jax.random.normal(key_list[1], (2, D), jnp.float32), 0.5, 1.5),
        "query_key_value_weight": gaussian(key_list[2], (3, D, D), D ** -0.5, 0.125, ((2, 8),)),
        "output_weight": gaussian(key_list[3], (D, D), D ** -0.5, 0.125, ((0, 8),)),
        "gate_up_weight": gaussian(key_list[4], (2, D, FF), D ** -0.5, 0.125, ((2, 8),)),
        "down_weight": gaussian(key_list[5], (FF, D), FF ** -0.5, 0.078125, ((0, 8),)),
        "a_in": gaussian(key_list[6], (6, D, RANK), D ** -0.5, 0.125, ((1, 32),), jnp.float32),
        "a_down": gaussian(key_list[7], (FF, RANK), FF ** -0.5, 0.078125, ((0, 32),), jnp.float32),
        "b_dmodel": gaussian(key_list[8], (5, RANK, D), (16 * RANK) ** -0.5, 0.375, ((2, 32),), jnp.float32),
        "b_hidden": gaussian(key_list[9], (2, RANK, FF), (16 * RANK) ** -0.5, 0.375, ((2, 32),), jnp.float32),
        "m_dmodel": draw_m_dmodel(jax.random.fold_in(key_list[15], 71), 0),
        "m_hidden": jnp.clip(jnp.exp(math.log(1.6) - 0.82667861 * jax.random.uniform(key_list[11], (2, FF), jnp.float32) ** block_levels(key_list[11], (2, FF), ((1, 32),), -0.2, 0.2)), 0.7, 1.6),
        "segment_ids": draw_segment_ids(jax.random.fold_in(key_list[15], 71), 0),
        "valid_mask": draw_valid_mask(jax.random.fold_in(key_list[15], 71), 0),
        "cotangent": gaussian(key_list[14], (TOKENS, D), 1.0, 6.0, ((0, 4), (1, 8))),
    }


@jax.custom_vjp
def low(v):
    return lax.optimization_barrier(v.astype(jnp.bfloat16)).astype(jnp.float32)

@jax.custom_vjp
def low_back(v):
    return v

def low_keep(v):
    return (low(v), None)

def low_pass(kept, grad):
    return (grad,)

def back_keep(v):
    return (v, None)

def back_low(kept, grad):
    return (low(grad),)
low.defvjp(low_keep, low_pass)
low_back.defvjp(back_keep, back_low)
EPSILON = 1e-05
ADAPTER_SCALE = 2.0
ROPE_BASE = 10000.0
MASKED = -1e+30

def matrix_product(left, right):
    return jnp.dot(left, right, precision=lax.Precision.HIGHEST)

def positions(segments):
    index = jnp.broadcast_to(jnp.arange(segments.shape[1], dtype=jnp.int32)[None, :], segments.shape)
    earlier = jnp.concatenate([segments[:, :1] - 1, segments[:, :-1]], axis=1)
    starts = lax.cummax(jnp.where(segments != earlier, index, 0), axis=1)
    return index - starts

def rope_tables(segments):
    half_size = HEAD // 2
    frequency = ROPE_BASE ** (-(jnp.arange(half_size, dtype=jnp.float32) * (2.0 / HEAD)))
    angles = positions(segments).astype(jnp.float32)[..., None] * frequency
    angles = jnp.concatenate([angles, angles], axis=-1)
    return (jnp.cos(angles)[:, :, None, :], jnp.sin(angles)[:, :, None, :])

def rotate(values):
    half_size = values.shape[-1] // 2
    return jnp.concatenate([-values[..., half_size:], values[..., :half_size]], axis=-1)

def rotary(values, cosine, sine):
    return values * cosine + rotate(values) * sine

def rms_scale(stream):
    return lax.rsqrt(lax.optimization_barrier(jnp.mean(stream * stream, axis=-1, keepdims=True)) + EPSILON)

def dora_finish(inputs, frozen_product, weight_matrix, first_adapter, second_adapter, magnitude):
    merged_weight = weight_matrix + ADAPTER_SCALE * matrix_product(first_adapter, second_adapter)
    column_norm = jnp.sqrt(lax.optimization_barrier(jnp.sum(merged_weight * merged_weight, axis=0)))
    adapter_product = low_back(low(matrix_product(inputs, first_adapter)))
    unscaled_output = frozen_product + ADAPTER_SCALE * matrix_product(adapter_product, second_adapter)
    return low_back(unscaled_output) * (magnitude / column_norm)

def column_group(inputs, weights, adapters_a, adapters_b, magnitudes):
    block_width = weights[0].shape[1] // N_MP
    pieces = [[] for weight_matrix in weights]
    for block in range(N_MP):
        copy_in = low_back(inputs)
        for index in range(len(weights)):
            pieces[index].append(matrix_product(copy_in, weights[index][:, block * block_width:(block + 1) * block_width]))
    results = []
    for index in range(len(weights)):
        results.append(dora_finish(inputs, jnp.concatenate(pieces[index], axis=1), weights[index], adapters_a[index], adapters_b[index], magnitudes[index]))
    return results

def row_single(inputs, weight_matrix, first_adapter, second_adapter, magnitude):
    block_width = weight_matrix.shape[0] // N_MP
    frozen_product = low(matrix_product(inputs[:, 0:block_width], weight_matrix[0:block_width]))
    for block in range(1, N_MP):
        lower = block * block_width
        frozen_product = frozen_product + low(matrix_product(inputs[:, lower:lower + block_width], weight_matrix[lower:lower + block_width]))
    return dora_finish(inputs, frozen_product, weight_matrix, first_adapter, second_adapter, magnitude)

def attend_one(item):
    query_row, key_rows, value_rows, segment_row, valid_row = item
    index = jnp.arange(SEQ, dtype=jnp.int32)
    scores = low_back(matrix_product(query_row, key_rows.T) * HEAD ** (-0.5))
    allowed = (segment_row[:, None] == segment_row[None, :]) & (index[None, :] <= index[:, None])
    allowed = allowed & ((valid_row[None, :] > 0) | (index[None, :] == index[:, None]))
    masked = jnp.where(allowed, scores, MASKED)
    maxima = lax.optimization_barrier(jnp.max(masked, axis=-1, keepdims=True))
    weights = jnp.exp(masked - maxima)
    probs = weights / lax.optimization_barrier(jnp.sum(weights, axis=-1, keepdims=True))
    return matrix_product(low(probs), value_rows)

def layer(stream, masters, frozen, segments, valid):
    query_key_value_weight, output_weight, gate_up_weight, down_weight, gains = frozen
    a_in, a_down, b_dmodel, b_hidden, m_dmodel, m_hidden = [low(item) for item in masters]
    row_count = segments.shape[0]
    normed_input = low(stream * rms_scale(stream) * gains[0])
    y_query, y_key, y_value = column_group(normed_input, [query_key_value_weight[0], query_key_value_weight[1], query_key_value_weight[2]], [a_in[0], a_in[1], a_in[2]], [b_dmodel[0], b_dmodel[1], b_dmodel[2]], [m_dmodel[0], m_dmodel[1], m_dmodel[2]])
    cosine, sine = rope_tables(segments)
    shape_four = (row_count, SEQ, H, HEAD)
    query = low(rotary(y_query.reshape(shape_four), cosine, sine))
    keys = low(rotary(y_key.reshape(shape_four), cosine, sine))
    values = low(y_value.reshape(shape_four))

    def heads_first(array):
        return array.transpose(0, 2, 1, 3).reshape(row_count * H, SEQ, HEAD)
    attended = lax.map(jax.checkpoint(attend_one), (heads_first(query), heads_first(keys), heads_first(values), jnp.repeat(segments, H, axis=0), jnp.repeat(valid, H, axis=0)))
    attended = attended.reshape(row_count, H, SEQ, HEAD).transpose(0, 2, 1, 3).reshape(row_count * SEQ, D)
    attended = low_back(low(attended))
    middle = stream + row_single(attended, output_weight, a_in[3], b_dmodel[3], m_dmodel[3])
    normed_second = low(middle * rms_scale(middle) * gains[1])
    y_gate, y_up = column_group(normed_second, [gate_up_weight[0], gate_up_weight[1]], [a_in[4], a_in[5]], [b_hidden[0], b_hidden[1]], [m_hidden[0], m_hidden[1]])
    hidden = low(y_gate * jax.nn.sigmoid(y_gate) * y_up)
    return middle + row_single(hidden, down_weight, a_down, b_dmodel[4], m_dmodel[4])

def reference(tokens, norm_gains, query_key_value_weight, output_weight, gate_up_weight, down_weight, a_in, a_down, b_dmodel, b_hidden, m_dmodel, m_hidden, segment_ids, valid_mask, cotangent):
    frozen = (query_key_value_weight.astype(jnp.float32), output_weight.astype(jnp.float32), gate_up_weight.astype(jnp.float32), down_weight.astype(jnp.float32), norm_gains.astype(jnp.float32))
    masters = (a_in, a_down, b_dmodel, b_hidden, m_dmodel, m_hidden)
    group_tokens = ROWS_DEV * SEQ
    inputs = (tokens.reshape(N_DP, group_tokens, D), segment_ids.reshape(N_DP, ROWS_DEV, SEQ), valid_mask.reshape(N_DP, ROWS_DEV, SEQ), cotangent.reshape(N_DP, group_tokens, D))

    def step(totals, item):
        stream, segments, valid, cotan = item

        def forward(stream_in, adapters):
            return layer(stream_in, adapters, frozen, segments, valid)
        output, pullback = jax.vjp(forward, stream.astype(jnp.float32), masters)
        grad_stream, grad_masters = pullback(cotan.astype(jnp.float32))
        totals = tuple((total + grad for total, grad in zip(totals, grad_masters)))
        return (totals, (output.astype(jnp.bfloat16), grad_stream.astype(jnp.bfloat16)))
    zeros = tuple((jnp.zeros(item.shape, jnp.float32) for item in masters))
    totals, (outputs, grads) = lax.scan(step, zeros, inputs)
    return (outputs.reshape(TOKENS, D), grads.reshape(TOKENS, D), totals[0], totals[1], totals[2], totals[3], totals[4], totals[5])
```

```python
import functools

import jax
import jax.numpy as jnp
from jax import lax
from jax.experimental import pallas as pl
from jax.experimental.pallas import tpu as pltpu
from jax.sharding import PartitionSpec as P

D = 2048
HEAD = 128
FF = 5632
RANK = 16
SEGMENTS = 8
EPSILON = 1e-05
ROPE_BASE = 10000.0
MASKED = -1e30
ROW = 2
CHUNKS = 2
BQ = 256
BK = 256
F32 = jnp.float32
BF16 = jnp.bfloat16

NN = (((1,), (0,)), ((), ()))
NT = (((1,), (1,)), ((), ()))
TN = (((0,), (0,)), ((), ()))


def dot(a, b, dims=NN):
    return lax.dot_general(a, b, dims, preferred_element_type=F32)


def params(rank):
    return pltpu.CompilerParams(
        dimension_semantics=("arbitrary",) * rank, vmem_limit_bytes=56 * 2**20
    )


def cost(flops, moved, exps=0):
    return pl.CostEstimate(flops=int(flops), bytes_accessed=int(moved), transcendentals=int(exps))


def bytes_of(arrays):
    return sum(a.size * a.dtype.itemsize for a in arrays)


def fixed(shape):
    rank = len(shape)
    return pl.BlockSpec(shape, lambda *_: (0,) * rank, pipeline_mode=pl.Buffered(1))


def tiles(width, step=512):
    return [(at, min(step, width - at)) for at in range(0, width, step)]


def merge_columns(perm, own, other, adapter_a, adapter_b, gain, first):
    count, rows, width = own.shape
    blocks = perm.shape[0]
    size = rows // blocks
    local = adapter_b.shape[2]

    def body(perm_ref, own_ref, other_ref, a_ref, b_ref, gain_ref, v_ref, sq_ref):
        @pl.when(pl.program_id(0) == 0)
        def _():
            sq_ref[...] = jnp.zeros_like(sq_ref)

        for k in range(count):
            low = (first + k) * RANK
            product = dot(a_ref[:, low : low + RANK], b_ref[k])
            weight = jnp.concatenate([own_ref[k].astype(F32), other_ref[k].astype(F32)], axis=1)
            merged = weight + 2.0 * product
            sq_ref[k] += jnp.sum(merged * merged, axis=0, keepdims=True)
            v_ref[k] = (merged * gain_ref[...]).astype(BF16)

    return pl.pallas_call(
        body,
        out_shape=(
            jax.ShapeDtypeStruct((count, rows, local), BF16),
            jax.ShapeDtypeStruct((count, 1, local), F32),
        ),
        grid_spec=pltpu.PrefetchScalarGridSpec(
            num_scalar_prefetch=1,
            grid=(blocks,),
            in_specs=[
                pl.BlockSpec((count, size, width), lambda i, p: (0, p[i], 0)),
                pl.BlockSpec((count, size, width), lambda i, p: (0, p[i], 0)),
                pl.BlockSpec((size, adapter_a.shape[1]), lambda i, p: (i, 0)),
                fixed(adapter_b.shape),
                pl.BlockSpec((size, 1), lambda i, p: (i, 0)),
            ],
            out_specs=[
                pl.BlockSpec((count, size, local), lambda i, p: (0, i, 0)),
                pl.BlockSpec((count, 1, local), lambda i, p: (0, 0, 0)),
            ],
        ),
        compiler_params=params(1),
        cost_estimate=cost(4 * own.size * 64, 4 * bytes_of([own])),
        name="merge_columns",
    )(perm, own, other, adapter_a, adapter_b, gain)


def merge_rows(perm, own, other, adapter_a, adapter_b):
    height, columns = own.shape
    blocks = perm.shape[0]
    size = columns // blocks

    def body(perm_ref, own_ref, other_ref, a_ref, b_ref, v_ref, sq_ref):
        weight = jnp.concatenate([own_ref[...].astype(F32), other_ref[...].astype(F32)], axis=0)
        merged = weight + 2.0 * dot(a_ref[...], b_ref[...])
        sq_ref[...] = jnp.sum(merged * merged, axis=0, keepdims=True)
        v_ref[...] = merged.astype(BF16)

    return pl.pallas_call(
        body,
        out_shape=(
            jax.ShapeDtypeStruct((2 * height, columns), BF16),
            jax.ShapeDtypeStruct((1, columns), F32),
        ),
        grid_spec=pltpu.PrefetchScalarGridSpec(
            num_scalar_prefetch=1,
            grid=(blocks,),
            in_specs=[
                pl.BlockSpec((height, size), lambda i, p: (0, p[i])),
                pl.BlockSpec((height, size), lambda i, p: (0, p[i])),
                fixed(adapter_a.shape),
                pl.BlockSpec((RANK, size), lambda i, p: (0, i)),
            ],
            out_specs=[
                pl.BlockSpec((2 * height, size), lambda i, p: (0, i)),
                pl.BlockSpec((1, size), lambda i, p: (0, i)),
            ],
        ),
        compiler_params=params(1),
        cost_estimate=cost(4 * own.size * 64, 4 * bytes_of([own])),
        name="merge_rows",
    )(perm, own, other, adapter_a, adapter_b)


def inverse_rms(x):
    wide = x.astype(F32)
    return lax.rsqrt(jnp.sum(wide * wide, axis=1, keepdims=True) / D + EPSILON)


def project_qkv(parts, weights, low, scale, cosine, sine):
    rows, width = parts[0].shape
    local = weights.shape[2]
    bm = 256

    def body(*refs):
        part_refs = refs[: len(parts)]
        v_ref, a_ref, s_ref, cos_ref, sin_ref, out_ref, u_ref, r_ref = refs[len(parts) :]
        x = jnp.concatenate([ref[...] for ref in part_refs], axis=1)
        r = inverse_rms(x)
        r_ref[...] = jnp.broadcast_to(r, r_ref.shape)
        u_ref[...] = (dot(x, a_ref[...]) * r).astype(BF16)
        cos, sin = cos_ref[...], sin_ref[...]
        for k in range(3):
            y = dot(x, v_ref[k]) * r * s_ref[k]
            for at in range(0, local, HEAD):
                head = y[:, at : at + HEAD]
                if k < 2:
                    head = head * cos + pltpu.roll(head, HEAD // 2, 1) * sin
                out_ref[:, k * local + at : k * local + at + HEAD] = head.astype(BF16)

    outs = (
        jax.ShapeDtypeStruct((rows, 3 * local), BF16),
        jax.ShapeDtypeStruct((rows, 128), BF16),
        jax.ShapeDtypeStruct((rows, 128), F32),
    )
    return pl.pallas_call(
        body,
        out_shape=outs,
        grid=(rows // bm,),
        in_specs=[pl.BlockSpec((bm, width), lambda i: (i, 0))] * len(parts)
        + [
            fixed(weights.shape),
            fixed(low.shape),
            fixed(scale.shape),
            pl.BlockSpec((bm, HEAD), lambda i: (i, 0)),
            pl.BlockSpec((bm, HEAD), lambda i: (i, 0)),
        ],
        out_specs=[
            pl.BlockSpec((bm, 3 * local), lambda i: (i, 0)),
            pl.BlockSpec((bm, 128), lambda i: (i, 0)),
            pl.BlockSpec((bm, 128), lambda i: (i, 0)),
        ],
        compiler_params=params(1),
        cost_estimate=cost(6 * rows * D * local, bytes_of([*parts, weights, *outs])),
        name="project_qkv",
    )(*parts, weights, low, scale, cosine, sine)


def project_hidden(parts, weights, low, scale, down_low):
    rows, width = parts[0].shape
    local = weights.shape[2]
    bm = 256

    def body(*refs):
        part_refs = refs[: len(parts)]
        v_ref, a_ref, s_ref, d_ref, gate_ref, up_ref, hid_ref, u_ref, ud_ref, r_ref = refs[
            len(parts) :
        ]
        x = jnp.concatenate([ref[...] for ref in part_refs], axis=1)
        r = inverse_rms(x)
        r_ref[...] = jnp.broadcast_to(r, r_ref.shape)
        u_ref[...] = (dot(x, a_ref[...]) * r).astype(BF16)
        for at, size in tiles(local):
            cut = slice(at, at + size)
            gate = dot(x, v_ref[0, :, cut]) * r * s_ref[0, :, cut]
            up = dot(x, v_ref[1, :, cut]) * r * s_ref[1, :, cut]
            gate_ref[:, cut] = gate.astype(BF16)
            up_ref[:, cut] = up.astype(BF16)
            hid_ref[:, cut] = (gate * jax.nn.sigmoid(gate) * up).astype(BF16)
        ud_ref[...] = dot(hid_ref[...], d_ref[...]).astype(BF16)

    wide = jax.ShapeDtypeStruct((rows, local), BF16)
    outs = (
        wide,
        wide,
        wide,
        jax.ShapeDtypeStruct((rows, 128), BF16),
        jax.ShapeDtypeStruct((rows, 128), BF16),
        jax.ShapeDtypeStruct((rows, 128), F32),
    )
    return pl.pallas_call(
        body,
        out_shape=outs,
        grid=(rows // bm,),
        in_specs=[pl.BlockSpec((bm, width), lambda i: (i, 0))] * len(parts)
        + [fixed(weights.shape), fixed(low.shape), fixed(scale.shape), fixed(down_low.shape)],
        out_specs=[pl.BlockSpec((bm, local), lambda i: (i, 0))] * 3
        + [pl.BlockSpec((bm, 128), lambda i: (i, 0))] * 3,
        compiler_params=params(1),
        cost_estimate=cost(4 * rows * D * local, bytes_of([*parts, weights, *outs]), rows * local),
        name="project_hidden",
    )(*parts, weights, low, scale, down_low)


def hidden_backward(parts, down, down_scale, down_low, gate, up, scale):
    rows, width = parts[0].shape
    local = down.shape[0]
    bm = 256

    def body(*refs):
        part_refs = refs[: len(parts)]
        v_ref, ds_ref, b_ref, gate_ref, up_ref, s_ref, gg_ref, gu_ref, t_ref, in_ref, low_ref = refs[
            len(parts) :
        ]

        @pl.when(pl.program_id(0) == 0)
        def _():
            t_ref[...] = jnp.zeros_like(t_ref)

        raw = jnp.concatenate([ref[...] for ref in part_refs], axis=1).astype(F32)
        g = (raw * ds_ref[...]).astype(BF16)
        low_ref[...] = dot(g, b_ref[...], NT).astype(BF16)
        inner = jnp.zeros((bm, 1), F32)
        for at, size in tiles(local):
            cut = slice(at, at + size)
            back = dot(g, v_ref[cut, :], NT)
            y_gate = gate_ref[:, cut].astype(F32)
            y_up = up_ref[:, cut].astype(F32)
            sig = jax.nn.sigmoid(y_gate)
            act = y_gate * sig
            g_gate = back * y_up * (sig + act * (1.0 - sig))
            g_up = back * act
            dot_gate = g_gate * y_gate
            dot_up = g_up * y_up
            t_ref[0, :, cut] += jnp.sum(dot_gate, axis=0, keepdims=True)
            t_ref[1, :, cut] += jnp.sum(dot_up, axis=0, keepdims=True)
            inner += jnp.sum(dot_gate + dot_up, axis=1, keepdims=True)
            gg_ref[:, cut] = (g_gate * s_ref[0, :, cut]).astype(BF16)
            gu_ref[:, cut] = (g_up * s_ref[1, :, cut]).astype(BF16)
        in_ref[...] = jnp.broadcast_to(inner, in_ref.shape)

    wide = jax.ShapeDtypeStruct((rows, local), BF16)
    outs = (
        wide,
        wide,
        jax.ShapeDtypeStruct((2, 1, local), F32),
        jax.ShapeDtypeStruct((rows, 128), F32),
        jax.ShapeDtypeStruct((rows, 128), BF16),
    )
    return pl.pallas_call(
        body,
        out_shape=outs,
        grid=(rows // bm,),
        in_specs=[pl.BlockSpec((bm, width), lambda i: (i, 0))] * len(parts)
        + [fixed(down.shape), fixed(down_scale.shape), fixed(down_low.shape)]
        + [pl.BlockSpec((bm, local), lambda i: (i, 0))] * 2
        + [fixed(scale.shape)],
        out_specs=[pl.BlockSpec((bm, local), lambda i: (i, 0))] * 2
        + [
            pl.BlockSpec((2, 1, local), lambda i: (0, 0, 0)),
            pl.BlockSpec((bm, 128), lambda i: (i, 0)),
            pl.BlockSpec((bm, 128), lambda i: (i, 0)),
        ],
        compiler_params=params(1),
        cost_estimate=cost(
            2 * rows * D * local, bytes_of([*parts, down, gate, up, *outs]), rows * local
        ),
        name="hidden_backward",
    )(*parts, down, down_scale, down_low, gate, up, scale)


def matmul(lefts, rights, dims, at, step, count, width, add=None, add_at=0, kind=BF16):
    rows = lefts[0].shape[0]
    bm = min(512, rows)
    rank = len(lefts)

    def body(*refs):
        total = None
        for left, right in zip(refs[:rank], refs[rank : 2 * rank]):
            value = dot(left[...], right[...], dims)
            total = value if total is None else total + value
        if add is not None:
            total = total + refs[2 * rank][...].astype(F32)
        refs[-1][...] = total.astype(kind)

    specs = [pl.BlockSpec((bm, a.shape[1]), lambda p, m: (m, 0)) for a in lefts]
    arrays = []
    depth = 0
    for array, index in rights:
        if dims is NT:
            size = array.shape[-1]
            if index is None:
                specs.append(pl.BlockSpec((width, size), lambda p, m: (at + step * p, 0)))
            else:
                specs.append(
                    pl.BlockSpec(
                        (None, width, size), lambda p, m, k=index: (k, at + step * p, 0)
                    )
                )
        else:
            size = array.shape[-2]
            specs.append(pl.BlockSpec((size, width), lambda p, m: (0, at + step * p)))
        arrays.append(array)
        depth += size
    if add is not None:
        specs.append(pl.BlockSpec((None, bm, width), lambda p, m: (add_at + p, m, 0)))
        arrays.append(add)
    out = jax.ShapeDtypeStruct((count, rows, width), kind)
    return pl.pallas_call(
        body,
        out_shape=out,
        grid=(count, rows // bm),
        in_specs=specs,
        out_specs=pl.BlockSpec((None, bm, width), lambda p, m: (p, m, 0)),
        compiler_params=params(2),
        cost_estimate=cost(
            2 * count * rows * width * depth,
            count * (bytes_of(lefts) + 2 * width * depth) + bytes_of([out]),
        ),
        name="matmul_add",
    )(*lefts, *arrays)


def visible(start, query, key, last):
    return (key >= start) & ((key <= jnp.minimum(query, last)) | (key == query))


def attention_forward(table, qkv_q, keys, values, starts, offset):
    rows = qkv_q.shape[0]
    length, local = keys.shape
    heads = local // HEAD
    factor = HEAD**-0.5

    def body(table_ref, q_ref, k_ref, v_ref, start_ref, out_ref, lse_ref):
        i = pl.program_id(1)
        base = offset + i * BQ
        q = q_ref[...]
        start = start_ref[...]
        query = base + lax.broadcasted_iota(jnp.int32, (1, BQ), 1)
        last = table_ref[0] - 1

        def step(j, carry):
            top, total, acc = carry
            at = pl.multiple_of(j * BK, BK)
            scores = dot(k_ref[pl.ds(at, BK), :], q, NT) * factor
            key = at + lax.broadcasted_iota(jnp.int32, (BK, BQ), 0)
            scores = jnp.where(visible(start, query, key, last), scores, MASKED)
            higher = jnp.maximum(top, jnp.max(scores, axis=0, keepdims=True))
            fade = jnp.exp(top - higher)
            weights = jnp.exp(scores - higher)
            total = total * fade + jnp.sum(weights, axis=0, keepdims=True)
            acc = acc * fade + dot(v_ref[pl.ds(at, BK), :], weights.astype(BF16), TN)
            return higher, total, acc

        empty = (
            jnp.full((1, BQ), MASKED, F32),
            jnp.zeros((1, BQ), F32),
            jnp.zeros((HEAD, BQ), F32),
        )
        block = offset // BQ + i
        top, total, acc = lax.fori_loop(table_ref[1 + block], block + 1, step, empty)
        out_ref[...] = jnp.transpose(acc / total).astype(BF16)
        lse_ref[...] = top + jnp.log(total)

    outs = (
        jax.ShapeDtypeStruct((rows, local), BF16),
        jax.ShapeDtypeStruct((heads, 1, rows), F32),
    )
    first = offset // BQ
    return pl.pallas_call(
        body,
        out_shape=outs,
        grid_spec=pltpu.PrefetchScalarGridSpec(
            num_scalar_prefetch=1,
            grid=(heads, rows // BQ),
            in_specs=[
                pl.BlockSpec((BQ, HEAD), lambda h, i, t: (i, h)),
                pl.BlockSpec((length, HEAD), lambda h, i, t: (0, h)),
                pl.BlockSpec((length, HEAD), lambda h, i, t: (0, h)),
                pl.BlockSpec((1, BQ), lambda h, i, t: (0, first + i)),
            ],
            out_specs=[
                pl.BlockSpec((BQ, HEAD), lambda h, i, t: (i, h)),
                pl.BlockSpec((None, 1, BQ), lambda h, i, t: (h, 0, i)),
            ],
        ),
        compiler_params=params(2),
        cost_estimate=cost(
            2 * rows * length * local, bytes_of([keys, values, *outs]), rows * length * heads // 2
        ),
        name="attention_forward",
    )(table, qkv_q, keys, values, starts)


def attention_backward(table, qkv, grad, attended, lse, starts, cosine, sine, scale):
    length = qkv.shape[0]
    local = grad.shape[1]
    heads = local // HEAD
    factor = HEAD**-0.5
    blocks = length // BQ

    def body(table_ref, q_ref, k_ref, v_ref, g_ref, att_ref, lse_ref, start_ref, cos_ref, sin_ref, s_ref, gq_ref, gk_ref, gv_ref, t_ref, in_ref, dk_ref, dv_ref):
        last = table_ref[0] - 1
        dk_ref[...] = jnp.zeros_like(dk_ref)
        dv_ref[...] = jnp.zeros_like(dv_ref)
        t_ref[...] = jnp.zeros_like(t_ref)

        @pl.when(pl.program_id(0) == 0)
        def _():
            in_ref[...] = jnp.zeros_like(in_ref)

        def back(values, here):
            return values * cos_ref[here, :] - pltpu.roll(values, HEAD // 2, 1) * sin_ref[here, :]

        def per_query(i, nothing):
            here = pl.ds(pl.multiple_of(i * BQ, BQ), BQ)
            q, g = q_ref[here, :], g_ref[here, :]
            start = start_ref[:, here]
            total = lse_ref[:, here]
            pairs = g.astype(F32) * att_ref[here, :].astype(F32)
            delta = jnp.sum(jnp.transpose(pairs), axis=0, keepdims=True)
            query = i * BQ + lax.broadcasted_iota(jnp.int32, (1, BQ), 1)

            def step(j, dq):
                at = pl.multiple_of(j * BK, BK)
                there = pl.ds(at, BK)
                k, v = k_ref[there, :], v_ref[there, :]
                scores = dot(k, q, NT) * factor
                key = at + lax.broadcasted_iota(jnp.int32, (BK, BQ), 0)
                seen = visible(start, query, key, last)
                weights = jnp.exp(jnp.where(seen, scores - total, MASKED))
                slopes = (weights * (dot(v, g, NT) - delta)).astype(BF16)
                dv_ref[there, :] += dot(weights.astype(BF16), g)
                dk_ref[there, :] += dot(slopes, q)
                return dq + dot(slopes, k, TN)

            dq = lax.fori_loop(table_ref[1 + i], i + 1, step, jnp.zeros((BQ, HEAD), F32))
            gy = back(dq * factor, here)
            both = gy * back(q.astype(F32), here)
            t_ref[0] += jnp.sum(both, axis=0, keepdims=True)
            in_ref[here, :] += both
            gq_ref[here, :] = (gy * s_ref[0]).astype(BF16)
            return nothing

        lax.fori_loop(0, blocks, per_query, 0)

        def per_key(i, nothing):
            here = pl.ds(pl.multiple_of(i * BQ, BQ), BQ)
            gy = back(dk_ref[here, :] * factor, here)
            both = gy * back(k_ref[here, :].astype(F32), here)
            t_ref[1] += jnp.sum(both, axis=0, keepdims=True)
            gk_ref[here, :] = (gy * s_ref[1]).astype(BF16)
            gv = dv_ref[here, :]
            more = gv * v_ref[here, :].astype(F32)
            t_ref[2] += jnp.sum(more, axis=0, keepdims=True)
            gv_ref[here, :] = (gv * s_ref[2]).astype(BF16)
            in_ref[here, :] += both + more
            return nothing

        lax.fori_loop(0, blocks, per_key, 0)

    column = jax.ShapeDtypeStruct((length, local), BF16)
    outs = (
        column,
        column,
        column,
        jax.ShapeDtypeStruct((3, 1, local), F32),
        jax.ShapeDtypeStruct((length, HEAD), F32),
    )
    per_head = pl.BlockSpec((length, HEAD), lambda h, t: (0, h))
    return pl.pallas_call(
        body,
        out_shape=outs,
        grid_spec=pltpu.PrefetchScalarGridSpec(
            num_scalar_prefetch=1,
            grid=(heads,),
            in_specs=[
                per_head,
                pl.BlockSpec((length, HEAD), lambda h, t: (0, heads + h)),
                pl.BlockSpec((length, HEAD), lambda h, t: (0, 2 * heads + h)),
                per_head,
                per_head,
                pl.BlockSpec((None, 1, length), lambda h, t: (h, 0, 0)),
                fixed(starts.shape),
                fixed(cosine.shape),
                fixed(sine.shape),
                pl.BlockSpec((3, 1, HEAD), lambda h, t: (0, 0, h)),
            ],
            out_specs=[
                per_head,
                per_head,
                per_head,
                pl.BlockSpec((3, 1, HEAD), lambda h, t: (0, 0, h)),
                pl.BlockSpec((length, HEAD), lambda h, t: (0, 0)),
            ],
            scratch_shapes=[pltpu.VMEM((length, HEAD), F32), pltpu.VMEM((length, HEAD), F32)],
        ),
        compiler_params=params(1),
        cost_estimate=cost(
            5 * length * length * local, bytes_of([qkv, grad, *outs]), length * length * heads // 2
        ),
        name="attention_backward",
    )(table, qkv, qkv, qkv, grad, attended, lse, starts, cosine, sine, scale)


def layer(
    n_dp,
    n_mp,
    tokens,
    norm_gains,
    query_key_value_weight,
    output_weight,
    gate_up_weight,
    down_weight,
    a_in,
    a_down,
    b_dmodel,
    b_hidden,
    m_dmodel,
    m_hidden,
    segment_ids,
    valid_mask,
    cotangent,
):
    length = segment_ids.shape[1]
    block = D // n_mp
    width = 2 * block
    hidden = FF // n_mp
    n_hi = n_mp // 4
    positions = 2 * n_hi
    chunk = length // CHUNKS
    me = lax.axis_index("mp")
    row = (me // ROW) % 2
    high_masks = [4 << k for k in range(n_hi.bit_length() - 1)]
    masks = [
        ((pos >> 1) << 2) | (side << 1) | (pos & 1) for pos in range(positions) for side in range(2)
    ]
    place_of = [masks.index(k) for k in range(n_mp)]
    perm = me ^ jnp.array(masks, jnp.int32)

    def swapped(blocks):
        for k in range(n_mp.bit_length() - 1):
            bit = (me >> k) % 2 == 1
            blocks = [jnp.where(bit, blocks[i ^ (1 << k)], b) for i, b in enumerate(blocks)]
        return blocks

    def to_relative(values):
        blocks = swapped([values[:, i * block : (i + 1) * block] for i in range(n_mp)])
        return jnp.concatenate([blocks[k] for k in masks], axis=1)

    def flip(values, mask):
        return lax.ppermute(values, "mp", [(i, i ^ mask) for i in range(n_mp)])

    def gather(values):
        far = [values]
        for mask in high_masks:
            far = far + [flip(v, mask) for v in far]
        return [v for f in far for v in (f, flip(f, 1))]

    def total(values):
        for mask in [1, *high_masks]:
            values = values + flip(values, mask)
        return values

    def total_relative(values):
        lead = values.shape[:-1]
        for mask in [1, *high_masks]:
            bit = 1 if mask == 1 else mask >> 1
            cut = (*lead, positions // (2 * bit), 2, bit * width)
            theirs = flip(values, mask).reshape(cut)
            theirs = jnp.concatenate([theirs[..., 1:2, :], theirs[..., 0:1, :]], axis=-2)
            values = (values.reshape(cut) + theirs).reshape(values.shape)
        return values

    def reduce_far(near, far):
        blocks = [near, *far]
        for mask in reversed(high_masks):
            half = len(blocks) // 2
            sent = [flip(b.astype(BF16), mask) for b in blocks[half:]]
            blocks = [a.astype(F32) + b.astype(F32) for a, b in zip(blocks[:half], sent)]
        return blocks[0]

    def product_scatter(lefts, rights, dims):
        odd = matmul(lefts, rights, dims, 1, 2, n_hi, width)
        theirs = flip(odd, 1)
        far = []
        if n_hi > 1:
            far = list(matmul(lefts, rights, dims, 2, 2, n_hi - 1, width, theirs, 1))
        near = matmul(lefts, rights, dims, 0, 2, 1, width, theirs, 0, F32)[0]
        return reduce_far(near, far)

    def my_row(values):
        return lax.dynamic_slice_in_dim(values, row * length, length, 0)

    def other_row(values):
        return lax.dynamic_slice_in_dim(values, (1 - row) * length, length, 0)

    def to_row(values):
        return jnp.concatenate([my_row(values), flip(other_row(values), ROW)], axis=1)

    def from_row(values):
        mine, theirs = values[:, :block], flip(values[:, block:], ROW)
        return jnp.where(
            row == 0,
            jnp.concatenate([mine, theirs], axis=0),
            jnp.concatenate([theirs, mine], axis=0),
        )

    def cut(values):
        return [values[c * chunk : (c + 1) * chunk] for c in range(CHUNKS)]

    stream = to_row(tokens)
    x_parts = [gather(v) for v in cut(stream)]
    thin, broad = a_in.shape[1], a_down.shape[0]
    packed = jnp.concatenate(
        [
            jnp.pad(
                jnp.concatenate(
                    [
                        jnp.transpose(a_in, (0, 2, 1)).reshape(6 * RANK, thin),
                        b_dmodel.reshape(5 * RANK, thin),
                        m_dmodel,
                    ],
                    axis=0,
                ),
                ((0, 0), (0, broad - thin)),
            ),
            jnp.transpose(a_down),
            b_hidden.reshape(2 * RANK, broad),
            m_hidden,
        ],
        axis=0,
    ).astype(BF16)
    model_rows = 11 * RANK + 5
    gathered = lax.all_gather(packed, ("dp", "mp"), axis=0)
    model = jnp.transpose(gathered[:, :model_rows, :thin], (1, 0, 2)).reshape(model_rows, D)
    model = to_relative(model)
    wide = jnp.transpose(gathered[:, model_rows:, :], (1, 0, 2)).reshape(3 * RANK + 2, n_mp, hidden)
    wide = jnp.concatenate(
        [lax.dynamic_index_in_dim(wide, i, 1, False) for i in (me, me ^ ROW)], axis=1
    )

    qkv_other = flip(query_key_value_weight, ROW)
    out_other = flip(output_weight, ROW)
    grad_output = to_row(cotangent)
    gate_up_other = flip(gate_up_weight, ROW)
    down_other = flip(down_weight, ROW)
    cot_parts = [gather(v) for v in cut(grad_output)]

    segments = lax.dynamic_slice_in_dim(segment_ids, row, 1, 0)
    valid = lax.dynamic_slice_in_dim(valid_mask, row, 1, 0)
    starts = jnp.zeros_like(segments)
    for s in range(SEGMENTS):
        count = jnp.sum((segments == s).astype(jnp.int32))
        starts = starts + jnp.where(segments > s, count, 0)
    table = jnp.concatenate([jnp.sum(valid, axis=1), starts[0, ::BQ] // BK])
    index = jnp.arange(length, dtype=jnp.int32)[None, :]
    frequency = ROPE_BASE ** (-(jnp.arange(HEAD // 2, dtype=F32) * (2.0 / HEAD)))
    angles = (index - starts)[0].astype(F32)[:, None] * frequency
    cos, sin = jnp.cos(angles), jnp.sin(angles)
    cosine = jnp.concatenate([cos, cos], axis=1)
    sine = jnp.concatenate([-sin, sin], axis=1)

    low_a = jnp.transpose(model[: 6 * RANK])
    model_b = [model[(6 + k) * RANK : (7 + k) * RANK] for k in range(5)]
    model_m = model[11 * RANK :].astype(F32)
    down_a = jnp.transpose(wide[:RANK])
    hidden_b = wide[RANK : 3 * RANK].reshape(2, RANK, 2 * hidden)
    hidden_m = wide[3 * RANK :].astype(F32)
    gains = to_relative(norm_gains)
    gain_columns = [gains[k].reshape(D, 1) for k in range(2)]
    lane = ((0, 0), (0, 128 - 6 * RANK))
    low_in = [jnp.pad((low_a.astype(F32) * g).astype(BF16), lane) for g in gain_columns]
    qkv_b = jnp.stack([b[:, :width] for b in model_b[:3]])
    qkv_v, qkv_sq = merge_columns(
        perm, query_key_value_weight, qkv_other, low_a, qkv_b, gain_columns[0], 0
    )
    qkv_m = model_m[:3, :width].reshape(3, 1, width)
    qkv_scale = qkv_m * lax.rsqrt(qkv_sq)
    out_a = low_a[:width, 3 * RANK : 4 * RANK]
    out_v, out_sq = merge_rows(perm, output_weight, out_other, out_a, model_b[3])
    gu_v, gu_sq = merge_columns(
        perm, gate_up_weight, gate_up_other, low_a, hidden_b, gain_columns[1], 4
    )
    gu_m = hidden_m.reshape(2, 1, 2 * hidden)
    gu_scale = gu_m * lax.rsqrt(gu_sq)
    down_v, down_sq = merge_rows(perm, down_weight, down_other, down_a, model_b[4])
    row_sq = total_relative(jnp.concatenate([out_sq, down_sq], axis=0))
    row_m = model_m[3:5]
    row_scale = row_m * lax.rsqrt(row_sq)
    out_scale, down_scale = row_scale[0:1], row_scale[1:2]

    qkv, qkv_u, r1, attended, lse = [], [], [], [], []
    keys, values = [], []
    cos_cut, sin_cut = cut(cosine), cut(sine)
    for c in range(CHUNKS):
        o, u, r = project_qkv(x_parts[c], qkv_v, low_in[0], qkv_scale, cos_cut[c], sin_cut[c])
        qkv.append(o)
        qkv_u.append(u)
        r1.append(r)
        keys.append(o[:, width : 2 * width])
        values.append(o[:, 2 * width :])
        att, l = attention_forward(
            table, o, jnp.concatenate(keys), jnp.concatenate(values), starts, c * chunk
        )
        attended.append(att)
        lse.append(l)
    middle, out_y, h_parts = [], [], []
    stream_cut, cot_cut = cut(stream), cut(grad_output)
    for c in range(CHUNKS):
        y = product_scatter([attended[c]], [(out_v, None)], NN) * out_scale[:, :width]
        out_y.append(y)
        h = stream_cut[c].astype(F32) + y
        middle.append(h)
        h_parts.append(gather(h.astype(BF16)))
    gate, up, hid, gu_u, down_u, r2 = [], [], [], [], [], []
    down_a_wide = jnp.pad(down_a, ((0, 0), (0, 128 - RANK)))
    for c in range(CHUNKS):
        g, u, h, ug, ud, r = project_hidden(h_parts[c], gu_v, low_in[1], gu_scale, down_a_wide)
        for bag, value in zip((gate, up, hid, gu_u, down_u, r2), (g, u, h, ug, ud, r)):
            bag.append(value)

    down_b_wide = jnp.pad(model_b[4], ((0, 128 - RANK), (0, 0)))
    g_gate, g_up, gu_t, inner2, down_gu = [], [], [], [], []
    for c in range(CHUNKS):
        outs = hidden_backward(
            cot_parts[c], down_v, down_scale, down_b_wide, gate[c], up[c], gu_scale
        )
        for bag, value in zip((g_gate, g_up, gu_t, inner2, down_gu), outs):
            bag.append(value)
    grad_middle, grad_out_parts = [], []
    for c in range(CHUNKS):
        sums = total(inner2[c][:, 0])
        g_x = product_scatter([g_gate[c], g_up[c]], [(gu_v, 0), (gu_v, 1)], NT)
        r = r2[c][:, :1]
        g = cot_cut[c].astype(F32) + r * g_x - middle[c] * (r * r * (sums / D)[:, None])
        grad_middle.append(g)
        grad_out_parts.append(gather((g * out_scale[:, :width]).astype(BF16)))
    grad_att = []
    for c in range(CHUNKS):
        rights = [out_v[:, p * width : (p + 1) * width] for p in range(positions)]
        grad_att.append(
            matmul(grad_out_parts[c], [(v, None) for v in rights], NT, 0, 1, 1, width)[0]
        )
    att_all = jnp.concatenate(attended)
    g_q, g_k, g_v, qkv_t, inner1 = attention_backward(
        table,
        jnp.concatenate(qkv),
        jnp.concatenate(grad_att),
        att_all,
        jnp.concatenate(lse, axis=2),
        starts,
        cosine,
        sine,
        qkv_scale,
    )
    sums1 = total(jnp.sum(inner1, axis=1))
    input_grad = []
    for c in range(CHUNKS):
        lefts = [cut(g)[c] for g in (g_q, g_k, g_v)]
        g_x = product_scatter(lefts, [(qkv_v, 0), (qkv_v, 1), (qkv_v, 2)], NT)
        r = r1[c][:, :1]
        s = cut(sums1)[c][:, None]
        g = grad_middle[c] + r * g_x - stream_cut[c].astype(F32) * (r * r * (s / D))
        input_grad.append(g.astype(BF16))

    down_y = [product_scatter([hid[c]], [(down_v, None)], NN) * down_scale[:, :width] for c in range(CHUNKS)]
    activations = jnp.concatenate(
        [(middle[c] + down_y[c]).astype(BF16) for c in range(CHUNKS)]
    )
    down_t = sum(jnp.sum(cot_cut[c].astype(F32) * down_y[c], axis=0) for c in range(CHUNKS))
    out_t = sum(jnp.sum(grad_middle[c] * out_y[c], axis=0) for c in range(CHUNKS))

    def over_tokens(left, right):
        return sum(dot(a, b, TN) for a, b in zip(left, right))

    def spread(lefts, parts):
        return jnp.concatenate(
            [over_tokens(lefts, [p[k] for p in parts]) for k in range(positions)], axis=1
        )

    def small(values):
        return values.astype(BF16)

    def to_natural(values):
        blocks = [values[:, i * block : (i + 1) * block] for i in place_of]
        return jnp.stack(swapped(blocks))

    def to_places(values):
        rows, both = values.shape
        half = both // 2
        holder = jnp.zeros((n_mp, rows, half), F32)
        holder = lax.dynamic_update_slice_in_dim(holder, values[None, :, :half], me, 0)
        return lax.dynamic_update_slice_in_dim(holder, values[None, :, half:], me ^ ROW, 0)

    def to_owner(values):
        rows, size = values.shape[1:]
        piece = size // n_dp
        v = jnp.transpose(values.reshape(n_mp, rows, n_dp, piece), (0, 2, 1, 3))
        v = v.reshape(n_dp, n_mp, rows, piece)
        mask, count = 1, n_mp
        while count > 1:
            v = v.reshape(n_dp, count // 2, 2, rows, piece)
            bit = (me // mask) % 2
            kept = lax.dynamic_index_in_dim(v, bit, 2, False)
            sent = lax.dynamic_index_in_dim(v, 1 - bit, 2, False)
            v = kept + flip(sent, mask)
            mask, count = mask * 2, count // 2
        v = v.reshape(n_dp, rows, piece)
        mine = lax.axis_index("dp")
        mask, count = 1, n_dp
        while count > 1:
            v = v.reshape(count // 2, 2, rows, piece)
            bit = (mine // mask) % 2
            kept = lax.dynamic_index_in_dim(v, bit, 1, False)
            sent = lax.dynamic_index_in_dim(v, 1 - bit, 1, False)
            v = kept + lax.ppermute(sent, "dp", [(i, i ^ mask) for i in range(n_dp)])
            mask, count = mask * 2, count // 2
        return v.reshape(rows, piece)

    gu_t = sum(gu_t)
    gu_coef = gu_t / gu_sq
    down_coef = jnp.concatenate(gather(down_t[None]), axis=1) / row_sq[1:2]
    gu_gu = []
    for c in range(CHUNKS):
        low = jnp.concatenate(
            [
                dot(g_gate[c], hidden_b[0], NT),
                dot(g_up[c], hidden_b[1], NT),
            ],
            axis=1,
        )
        gu_gu.append(small(low * r2[c][:, :1]))
    gu_ga = 2.0 * gains[1:2] * spread(gu_gu, h_parts)
    gu_na = jnp.concatenate(
        [dot(small(hidden_b[k] * gu_coef[k]), gu_v[k], NT) for k in range(2)], axis=0
    )
    gu_ga = gu_ga - 2.0 / gains[1:2] * gu_na
    low_back = [small(low_a.astype(F32) / g) for g in gain_columns]
    gu_gb = []
    for k, bag in enumerate((g_gate, g_up)):
        at = (4 + k) * RANK
        first = over_tokens([u[:, at : at + RANK] for u in gu_u], bag)
        second = dot(low_back[1][:, at : at + RANK], gu_v[k], TN) * gu_coef[k]
        gu_gb.append(2.0 * (first - second))
    down_ga = over_tokens(down_gu, hid)[:RANK] - dot(
        small(model_b[4] * down_coef), down_v, NT
    )
    down_gb = spread(down_u, cot_parts)[:RANK] * down_scale - dot(down_a, down_v, TN) * down_coef
    mlp_model = jnp.concatenate(
        [to_natural(jnp.concatenate([gu_ga, 2.0 * down_gb])), to_places((down_t / row_m[1, :width])[None])],
        axis=1,
    )
    mlp_wide = to_places(
        jnp.concatenate([2.0 * down_ga, *gu_gb, (gu_t / gu_m).reshape(2, 2 * hidden)])
    )
    mlp_model = to_owner(mlp_model)
    mlp_wide = to_owner(mlp_wide)

    qkv_coef = qkv_t / qkv_sq
    out_coef = jnp.concatenate(gather(out_t[None]), axis=1) / row_sq[0:1]
    grads = (g_q, g_k, g_v)
    low = jnp.concatenate([dot(grads[k], qkv_b[k], NT) for k in range(3)], axis=1)
    r1_all = jnp.concatenate(r1)[:, :1]
    qkv_gu = cut(small(low * r1_all))
    qkv_ga = 2.0 * gains[0:1] * spread(qkv_gu, x_parts)
    qkv_na = jnp.concatenate(
        [dot(small(qkv_b[k] * qkv_coef[k]), qkv_v[k], NT) for k in range(3)], axis=0
    )
    qkv_ga = qkv_ga - 2.0 / gains[0:1] * qkv_na
    u_all = jnp.concatenate(qkv_u)
    qkv_gb = []
    for k in range(3):
        at = k * RANK
        first = dot(u_all[:, at : at + RANK], grads[k], TN)
        second = dot(low_back[0][:, at : at + RANK], qkv_v[k], TN) * qkv_coef[k]
        qkv_gb.append(2.0 * (first - second))
    out_gu, out_u = [], []
    for c in range(CHUNKS):
        out_gu.append(
            small(
                sum(
                    dot(grad_out_parts[c][p], model_b[3][:, p * width : (p + 1) * width], NT)
                    for p in range(positions)
                )
            )
        )
        out_u.append(small(dot(attended[c], out_a)))
    out_ga = over_tokens(out_gu, attended) - dot(small(model_b[3] * out_coef), out_v, NT)
    out_gb = spread(out_u, grad_out_parts) - dot(out_a, out_v, TN) * out_coef
    att_model = jnp.concatenate(
        [
            to_natural(jnp.concatenate([qkv_ga, 2.0 * out_gb])),
            to_places(
                jnp.concatenate(
                    [
                        2.0 * out_ga,
                        *qkv_gb,
                        (qkv_t / qkv_m).reshape(3, width),
                        (out_t / row_m[0, :width])[None],
                    ]
                )
            ),
        ],
        axis=1,
    )
    att_model = to_owner(att_model)

    def stacked(values, count):
        return values.reshape(count, RANK, values.shape[1])

    rank4 = 4 * RANK
    grad_a = jnp.concatenate(
        [
            stacked(att_model[: 3 * RANK], 3),
            stacked(att_model[rank4 : rank4 + RANK], 1),
            stacked(mlp_model[: 2 * RANK], 2),
        ]
    )
    grad_b = jnp.concatenate(
        [
            stacked(att_model[rank4 + RANK : rank4 + 4 * RANK], 3),
            stacked(att_model[3 * RANK : rank4], 1),
            stacked(mlp_model[2 * RANK : 3 * RANK], 1),
        ]
    )
    grad_m = jnp.concatenate([att_model[rank4 + 4 * RANK :], mlp_model[3 * RANK :]])
    return (
        from_row(activations),
        from_row(jnp.concatenate(input_grad)),
        jnp.transpose(grad_a, (0, 2, 1)),
        jnp.transpose(mlp_wide[:RANK]),
        grad_b,
        stacked(mlp_wide[RANK : 3 * RANK], 2),
        grad_m,
        mlp_wide[3 * RANK :],
    )


def solution(mesh):
    in_specs = (
        P("dp", "mp"),
        P(),
        P(None, None, "mp"),
        P("mp", None),
        P(None, None, "mp"),
        P("mp", None),
        P(None, ("dp", "mp"), None),
        P(("dp", "mp"), None),
        P(None, None, ("dp", "mp")),
        P(None, None, ("dp", "mp")),
        P(None, ("dp", "mp")),
        P(None, ("dp", "mp")),
        P("dp", None),
        P("dp", None),
        P("dp", "mp"),
    )
    out_specs = (
        P("dp", "mp"),
        P("dp", "mp"),
        P(None, ("dp", "mp"), None),
        P(("dp", "mp"), None),
        P(None, None, ("dp", "mp")),
        P(None, None, ("dp", "mp")),
        P(None, ("dp", "mp")),
        P(None, ("dp", "mp")),
    )
    local = functools.partial(layer, mesh.shape["dp"], mesh.shape["mp"])
    return jax.shard_map(local, mesh=mesh, in_specs=in_specs, out_specs=out_specs, check_vma=False)
```

```python
import functools

import jax
import jax.numpy as jnp
from jax import lax
from jax.experimental import pallas as pl
from jax.experimental.pallas import tpu as pltpu
from jax.sharding import PartitionSpec as P

D = 2048
HEAD = 128
FF = 5632
RANK = 16
SEGMENTS = 8
EPSILON = 1e-05
ROPE_BASE = 10000.0
MASKED = -1e30
ROW = 2
CHUNKS = 2
BQ = 256
BK = 256
HEADS_FORWARD = 2
HEADS_BACKWARD = 2
COST = 0.15
F32 = jnp.float32
BF16 = jnp.bfloat16

NN = (((1,), (0,)), ((), ()))
NT = (((1,), (1,)), ((), ()))
TN = (((0,), (0,)), ((), ()))


def dot(a, b, dims=NN):
    return lax.dot_general(a, b, dims, preferred_element_type=F32)


def params(rank):
    return pltpu.CompilerParams(
        dimension_semantics=("arbitrary",) * rank, vmem_limit_bytes=56 * 2**20
    )


def cost(flops, moved, exps=0):
    return pl.CostEstimate(
        flops=int(flops * COST), bytes_accessed=int(moved * COST), transcendentals=int(exps * COST)
    )


def bytes_of(arrays):
    return sum(a.size * a.dtype.itemsize for a in arrays)


def fixed(shape):
    rank = len(shape)
    return pl.BlockSpec(shape, lambda *_: (0,) * rank, pipeline_mode=pl.Buffered(1))


def tiles(width, step=768):
    return [(at, min(step, width - at)) for at in range(0, width, step)]


def merge_columns(perm, own, pieces, adapter_a, adapter_b, gain, first):
    count, rows, width = own.shape
    blocks = perm.shape[0] - 1
    size = rows // blocks
    local = adapter_b.shape[2]
    parts = 2 * len(pieces[0])
    deep = blocks // parts

    def body(perm_ref, own_ref, *rest):
        piece_refs = rest[:parts]
        a_ref, b_ref, gain_ref, v_ref, sq_ref = rest[parts:]
        at = perm_ref[pl.program_id(0)] // deep
        swap = perm_ref[blocks] * (parts // 2)
        place = jnp.where(at >= swap, at - swap, at + parts // 2)

        @pl.when(pl.program_id(0) == 0)
        def _():
            sq_ref[...] = jnp.zeros_like(sq_ref)

        for k in range(count):
            low = (first + k) * RANK
            product = dot(a_ref[:, low : low + RANK], b_ref[k])
            other = piece_refs[0][k].astype(F32)
            for i in range(1, parts):
                other = jnp.where(place == i, piece_refs[i][k].astype(F32), other)
            weight = jnp.concatenate([own_ref[k].astype(F32), other], axis=1)
            merged = weight + 2.0 * product
            sq_ref[k] += jnp.sum(merged * merged, axis=0, keepdims=True)
            v_ref[k] = (merged * gain_ref[...]).astype(BF16)

    return pl.pallas_call(
        body,
        out_shape=(
            jax.ShapeDtypeStruct((count, rows, local), BF16),
            jax.ShapeDtypeStruct((count, 1, local), F32),
        ),
        grid_spec=pltpu.PrefetchScalarGridSpec(
            num_scalar_prefetch=1,
            grid=(blocks,),
            in_specs=[
                pl.BlockSpec((count, size, width), lambda i, p: (0, p[i], 0)),
                *[pl.BlockSpec((count, size, width), lambda i, p: (0, p[i] % deep, 0))] * parts,
                pl.BlockSpec((size, adapter_a.shape[1]), lambda i, p: (i, 0)),
                fixed(adapter_b.shape),
                pl.BlockSpec((size, 1), lambda i, p: (i, 0)),
            ],
            out_specs=[
                pl.BlockSpec((count, size, local), lambda i, p: (0, i, 0)),
                pl.BlockSpec((count, 1, local), lambda i, p: (0, 0, 0)),
            ],
        ),
        compiler_params=params(1),
        cost_estimate=cost(4 * own.size * 64, 4 * bytes_of([own])),
        name="merge_columns",
    )(perm, own, *pieces[0], *pieces[1], adapter_a, adapter_b, gain)


def merge_rows(perm, own, pieces, adapter_a, adapter_b, gain=None):
    count, height, columns = own.shape
    blocks = perm.shape[0] - 1
    size = columns // blocks
    whole = len(pieces) == 1
    parts = len(pieces[0])
    pieces = [p.reshape(-1, columns) for group in pieces for p in group]
    tall = pieces[0].shape[0]

    def body(perm_ref, own_ref, *rest):
        piece_refs = rest[: len(pieces)]
        a_ref, b_ref, *extra = rest[len(pieces) :]
        v_ref, sq_ref = extra[-2:]
        held = [ref[...].astype(F32) for ref in piece_refs]
        if not whole:
            first = perm_ref[blocks] == 0
            low, high = held[:parts], held[parts:]
            found = [
                [jnp.where(first, a, b) for a, b in zip(low, high)],
                [jnp.where(first, b, a) for a, b in zip(low, high)],
            ]
        if gain is not None:

            @pl.when(pl.program_id(0) == 0)
            def _():
                sq_ref[...] = jnp.zeros_like(sq_ref)

        for k in range(count):
            product = dot(a_ref[k], b_ref[k])
            if whole:
                others = held
            else:
                others = [*found[0], *found[1]] if count == 1 else found[k]
            places = [(0, own_ref[k].astype(F32))]
            for i, other in enumerate(others):
                places.append((height + i * tall, other))
            down = None
            for at, weight in places:
                part = slice(at, at + weight.shape[0])
                merged = weight + 2.0 * product[part]
                square = merged * merged
                if gain is None:
                    more = jnp.sum(square, axis=0, keepdims=True)
                    down = more if down is None else down + more
                else:
                    sq_ref[k, part] += jnp.sum(square, axis=1, keepdims=True)
                    merged = merged * extra[0][...]
                v_ref[k, part] = merged.astype(BF16)
            if gain is None:
                sq_ref[k] = down

    if gain is None:
        squares = jax.ShapeDtypeStruct((count, 1, columns), F32)
        squares_spec = pl.BlockSpec((count, 1, size), lambda i, p: (0, 0, i))
        extra_specs, extra = [], []
    else:
        squares = jax.ShapeDtypeStruct((count, 2 * height, 1), F32)
        squares_spec = pl.BlockSpec((count, 2 * height, 1), lambda i, p: (0, 0, 0))
        extra_specs, extra = [pl.BlockSpec((1, size), lambda i, p: (0, i))], [gain]
    return pl.pallas_call(
        body,
        out_shape=(jax.ShapeDtypeStruct((count, 2 * height, columns), BF16), squares),
        grid_spec=pltpu.PrefetchScalarGridSpec(
            num_scalar_prefetch=1,
            grid=(blocks,),
            in_specs=[
                pl.BlockSpec((count, height, size), lambda i, p: (0, 0, p[i])),
                *[pl.BlockSpec((tall, size), lambda i, p: (0, p[i]))] * len(pieces),
                fixed(adapter_a.shape),
                pl.BlockSpec((count, RANK, size), lambda i, p: (0, 0, i)),
                *extra_specs,
            ],
            out_specs=[
                pl.BlockSpec((count, 2 * height, size), lambda i, p: (0, 0, i)),
                squares_spec,
            ],
        ),
        compiler_params=params(1),
        cost_estimate=cost(4 * own.size * 64, 4 * bytes_of([own])),
        name="merge_rows",
    )(perm, own, *pieces, adapter_a, adapter_b, *extra)


def inverse_rms(x):
    wide = x.astype(F32)
    return lax.rsqrt(jnp.sum(wide * wide, axis=1, keepdims=True) / D + EPSILON)


def project_qkv(parts, weights, low, scale, cosine, sine):
    rows, width = parts[0].shape
    local = weights.shape[2]
    bm = min(512, rows)

    def body(*refs):
        part_refs = refs[: len(parts)]
        v_ref, a_ref, s_ref, cos_ref, sin_ref, out_ref, u_ref, r_ref = refs[len(parts) :]
        x = jnp.concatenate([ref[...] for ref in part_refs], axis=1)
        r = inverse_rms(x)
        r_ref[...] = jnp.broadcast_to(r, r_ref.shape)
        u_ref[...] = (dot(x, a_ref[...]) * r).astype(BF16)
        cos, sin = cos_ref[...], sin_ref[...]
        for k in range(3):
            y = dot(x, v_ref[k]) * r * s_ref[k]
            for at in range(0, local, HEAD):
                head = y[:, at : at + HEAD]
                if k < 2:
                    head = head * cos + pltpu.roll(head, HEAD // 2, 1) * sin
                out_ref[:, k * local + at : k * local + at + HEAD] = head.astype(BF16)

    outs = (
        jax.ShapeDtypeStruct((rows, 3 * local), BF16),
        jax.ShapeDtypeStruct((rows, 128), BF16),
        jax.ShapeDtypeStruct((rows, 128), F32),
    )
    return pl.pallas_call(
        body,
        out_shape=outs,
        grid=(rows // bm,),
        in_specs=[pl.BlockSpec((bm, width), lambda i: (i, 0))] * len(parts)
        + [
            fixed(weights.shape),
            fixed(low.shape),
            fixed(scale.shape),
            pl.BlockSpec((bm, HEAD), lambda i: (i, 0)),
            pl.BlockSpec((bm, HEAD), lambda i: (i, 0)),
        ],
        out_specs=[
            pl.BlockSpec((bm, 3 * local), lambda i: (i, 0)),
            pl.BlockSpec((bm, 128), lambda i: (i, 0)),
            pl.BlockSpec((bm, 128), lambda i: (i, 0)),
        ],
        compiler_params=params(1),
        cost_estimate=cost(6 * rows * D * local, bytes_of([*parts, weights, *outs])),
        name="project_qkv",
    )(*parts, weights, low, scale, cosine, sine)


def project_hidden(parts, weights, low, scale, down_low):
    rows, width = parts[0].shape
    local = weights.shape[1]
    bm = min(512, rows)

    def body(*refs):
        part_refs = refs[: len(parts)]
        v_ref, a_ref, s_ref, d_ref, gate_ref, up_ref, hid_ref, u_ref, ud_ref, r_ref = refs[
            len(parts) :
        ]
        x = jnp.concatenate([ref[...] for ref in part_refs], axis=1)
        r = inverse_rms(x)
        r_ref[...] = jnp.broadcast_to(r, r_ref.shape)
        u_ref[...] = (dot(x, a_ref[...]) * r).astype(BF16)
        for at, size in tiles(local):
            cut = slice(at, at + size)
            gate = dot(x, v_ref[0, cut, :], NT) * r * s_ref[0, :, cut]
            up = dot(x, v_ref[1, cut, :], NT) * r * s_ref[1, :, cut]
            gate_ref[:, cut] = gate.astype(BF16)
            up_ref[:, cut] = up.astype(BF16)
            hid_ref[:, cut] = (gate * jax.nn.sigmoid(gate) * up).astype(BF16)
        ud_ref[...] = dot(hid_ref[...], d_ref[...]).astype(BF16)

    wide = jax.ShapeDtypeStruct((rows, local), BF16)
    outs = (
        wide,
        wide,
        wide,
        jax.ShapeDtypeStruct((rows, 128), BF16),
        jax.ShapeDtypeStruct((rows, 128), BF16),
        jax.ShapeDtypeStruct((rows, 128), F32),
    )
    return pl.pallas_call(
        body,
        out_shape=outs,
        grid=(rows // bm,),
        in_specs=[pl.BlockSpec((bm, width), lambda i: (i, 0))] * len(parts)
        + [fixed(weights.shape), fixed(low.shape), fixed(scale.shape), fixed(down_low.shape)],
        out_specs=[pl.BlockSpec((bm, local), lambda i: (i, 0))] * 3
        + [pl.BlockSpec((bm, 128), lambda i: (i, 0))] * 3,
        compiler_params=params(1),
        cost_estimate=cost(4 * rows * D * local, bytes_of([*parts, weights, *outs]), rows * local),
        name="project_hidden",
    )(*parts, weights, low, scale, down_low)


def hidden_backward(parts, down, down_scale, down_low, gate, up, scale):
    rows, width = parts[0].shape
    local = down.shape[0]
    bm = min(512, rows)

    def body(*refs):
        part_refs = refs[: len(parts)]
        v_ref, ds_ref, b_ref, gate_ref, up_ref, s_ref, out_ref, t_ref, in_ref, low_ref = refs[
            len(parts) :
        ]

        @pl.when(pl.program_id(0) == 0)
        def _():
            t_ref[...] = jnp.zeros_like(t_ref)

        raw = jnp.concatenate([ref[...] for ref in part_refs], axis=1).astype(F32)
        g = (raw * ds_ref[...]).astype(BF16)
        low_ref[...] = dot(g, b_ref[...], NT).astype(BF16)
        inner = jnp.zeros((bm, 1), F32)
        for at, size in tiles(local):
            cut = slice(at, at + size)
            back = dot(g, v_ref[cut, :], NT)
            y_gate = gate_ref[:, cut].astype(F32)
            y_up = up_ref[:, cut].astype(F32)
            sig = jax.nn.sigmoid(y_gate)
            act = y_gate * sig
            g_gate = back * y_up * (sig + act * (1.0 - sig))
            g_up = back * act
            dot_gate = g_gate * y_gate
            dot_up = g_up * y_up
            t_ref[0, :, cut] += jnp.sum(dot_gate, axis=0, keepdims=True)
            t_ref[1, :, cut] += jnp.sum(dot_up, axis=0, keepdims=True)
            inner += jnp.sum(dot_gate + dot_up, axis=1, keepdims=True)
            out_ref[0, :, cut] = (g_gate * s_ref[0, :, cut]).astype(BF16)
            out_ref[1, :, cut] = (g_up * s_ref[1, :, cut]).astype(BF16)
        in_ref[...] = jnp.broadcast_to(inner, in_ref.shape)

    outs = (
        jax.ShapeDtypeStruct((2, rows, local), BF16),
        jax.ShapeDtypeStruct((2, 1, local), F32),
        jax.ShapeDtypeStruct((rows, 128), F32),
        jax.ShapeDtypeStruct((rows, 128), BF16),
    )
    return pl.pallas_call(
        body,
        out_shape=outs,
        grid=(rows // bm,),
        in_specs=[pl.BlockSpec((bm, width), lambda i: (i, 0))] * len(parts)
        + [fixed(down.shape), fixed(down_scale.shape), fixed(down_low.shape)]
        + [pl.BlockSpec((bm, local), lambda i: (i, 0))] * 2
        + [fixed(scale.shape)],
        out_specs=[
            pl.BlockSpec((2, bm, local), lambda i: (0, i, 0)),
            pl.BlockSpec((2, 1, local), lambda i: (0, 0, 0)),
            pl.BlockSpec((bm, 128), lambda i: (i, 0)),
            pl.BlockSpec((bm, 128), lambda i: (i, 0)),
        ],
        compiler_params=params(1),
        cost_estimate=cost(
            2 * rows * D * local, bytes_of([*parts, down, gate, up, *outs]), rows * local
        ),
        name="hidden_backward",
    )(*parts, down, down_scale, down_low, gate, up, scale)


def matmul(left, right, dims, half, width, add=None):
    count, rows, depth = left.shape
    size = D // 2
    bm = rows if count > 1 else min(512, rows)
    split = [width, size - width] if add is not None else [size]
    split = [v for v in split if v]

    def body(left_ref, right_ref, *rest):
        outs = rest[-1 - len(split) : -1] if count > 1 else rest[-len(split) :]
        k = pl.program_id(1)
        total = dot(left_ref[...], right_ref[...], dims)
        if count > 1:
            acc_ref = rest[-1]

            @pl.when(k == 0)
            def _():
                acc_ref[...] = total

            @pl.when((k > 0) & (k < count - 1))
            def _():
                acc_ref[...] += total

        def finish():
            value = total + acc_ref[...] if count > 1 else total
            if add is not None:
                value = value + rest[0][...].astype(F32)
            at = 0
            for out, columns in zip(outs, split):
                out[...] = value[:, at : at + columns].astype(out.dtype)
                at += columns

        if count > 1:
            pl.when(k == count - 1)(finish)
        else:
            finish()

    specs = [pl.BlockSpec((None, bm, depth), lambda m, k: (k, m, 0))]
    if dims is NT:
        specs.append(pl.BlockSpec((None, size, depth), lambda m, k: (k, half, 0)))
    else:
        specs.append(pl.BlockSpec((None, depth, size), lambda m, k: (k, 0, half)))
    arrays = [left, right]
    if add is not None:
        specs.append(pl.BlockSpec((bm, size), lambda m, k: (m, 0)))
        arrays.append(add)
    kinds = [F32, BF16] if add is not None else [BF16]
    outs = [jax.ShapeDtypeStruct((rows, v), kind) for v, kind in zip(split, kinds)]
    return pl.pallas_call(
        body,
        out_shape=outs,
        grid=(rows // bm, count),
        in_specs=specs,
        out_specs=[pl.BlockSpec((bm, v), lambda m, k: (m, 0)) for v in split],
        scratch_shapes=[pltpu.VMEM((bm, size), F32)] if count > 1 else [],
        compiler_params=params(2),
        cost_estimate=cost(
            2 * count * rows * size * depth,
            bytes_of([left, *outs]) + 2 * count * size * depth,
        ),
        name="matmul_half",
    )(*arrays)


def matmul_parts(parts, right):
    rows, width = parts[0].shape
    out = jax.ShapeDtypeStruct((rows, right.shape[0]), BF16)
    bm = min(512, rows)

    def body(*refs):
        left = jnp.concatenate([ref[...] for ref in refs[: len(parts)]], axis=1)
        refs[-1][...] = dot(left, refs[-2][...], NT).astype(BF16)

    return pl.pallas_call(
        body,
        out_shape=out,
        grid=(rows // bm,),
        in_specs=[pl.BlockSpec((bm, width), lambda m: (m, 0))] * len(parts) + [fixed(right.shape)],
        out_specs=pl.BlockSpec((bm, right.shape[0]), lambda m: (m, 0)),
        compiler_params=params(1),
        cost_estimate=cost(2 * rows * D * right.shape[0], bytes_of([*parts, right, out])),
        name="matmul_parts",
    )(*parts, right)


def visible(start, query, key, last):
    return (key >= start) & ((key <= jnp.minimum(query, last)) | (key == query))


def attention_forward(table, qkv_q, keys, values, starts, offset):
    rows = qkv_q.shape[0]
    length, local = keys.shape
    heads = local // HEAD
    together = min(HEADS_FORWARD, heads)
    wide = together * HEAD
    factor = HEAD**-0.5

    def body(table_ref, q_ref, k_ref, v_ref, start_ref, out_ref, lse_ref):
        i = pl.program_id(1)
        base = offset + i * BQ
        start = start_ref[...]
        query = base + lax.broadcasted_iota(jnp.int32, (1, BQ), 1)
        last = table_ref[0] - 1
        columns = [slice(h * HEAD, (h + 1) * HEAD) for h in range(together)]
        queries = [q_ref[:, c] for c in columns]

        def step(j, carry):
            at = pl.multiple_of(j * BK, BK)
            key = at + lax.broadcasted_iota(jnp.int32, (BK, BQ), 0)
            seen = visible(start, query, key, last)
            results = []
            for c, q, (top, total, acc) in zip(columns, queries, carry):
                scores = dot(k_ref[pl.ds(at, BK), c], q, NT) * factor
                scores = jnp.where(seen, scores, MASKED)
                higher = jnp.maximum(top, jnp.max(scores, axis=0, keepdims=True))
                fade = jnp.exp(top - higher)
                weights = jnp.exp(scores - higher)
                total = total * fade + jnp.sum(weights, axis=0, keepdims=True)
                acc = acc * fade + dot(v_ref[pl.ds(at, BK), c], weights.astype(BF16), TN)
                results.append((higher, total, acc))
            return tuple(results)

        empty = (
            jnp.full((1, BQ), MASKED, F32),
            jnp.zeros((1, BQ), F32),
            jnp.zeros((HEAD, BQ), F32),
        )
        block = offset // BQ + i
        carry = lax.fori_loop(table_ref[1 + block], block + 1, step, (empty,) * together)
        for h, (top, total, acc) in enumerate(carry):
            out_ref[:, columns[h]] = jnp.transpose(acc / total).astype(BF16)
            lse_ref[h] = top + jnp.log(total)

    outs = (
        jax.ShapeDtypeStruct((rows, local), BF16),
        jax.ShapeDtypeStruct((heads, 1, rows), F32),
    )
    first = offset // BQ
    return pl.pallas_call(
        body,
        out_shape=outs,
        grid_spec=pltpu.PrefetchScalarGridSpec(
            num_scalar_prefetch=1,
            grid=(heads // together, rows // BQ),
            in_specs=[
                pl.BlockSpec((BQ, wide), lambda h, i, t: (i, h)),
                pl.BlockSpec((length, wide), lambda h, i, t: (0, h)),
                pl.BlockSpec((length, wide), lambda h, i, t: (0, h)),
                pl.BlockSpec((1, BQ), lambda h, i, t: (0, first + i)),
            ],
            out_specs=[
                pl.BlockSpec((BQ, wide), lambda h, i, t: (i, h)),
                pl.BlockSpec((together, 1, BQ), lambda h, i, t: (h, 0, i)),
            ],
        ),
        compiler_params=params(2),
        cost_estimate=cost(
            2 * rows * length * local, bytes_of([keys, values, *outs]), rows * length * heads // 2
        ),
        name="attention_forward",
    )(table, qkv_q, keys, values, starts)


def attention_backward(table, qkv, grad, attended, lse, starts, cosine, sine, scale):
    length = qkv.shape[0]
    local = grad.shape[1]
    heads = local // HEAD
    together = min(HEADS_BACKWARD, heads)
    wide = together * HEAD
    steps = heads // together
    factor = HEAD**-0.5
    blocks = length // BQ
    columns = [slice(h * HEAD, (h + 1) * HEAD) for h in range(together)]

    def body(table_ref, q_ref, k_ref, v_ref, g_ref, att_ref, lse_ref, start_ref, cos_ref, sin_ref, s_ref, out_ref, t_ref, in_ref, dk_ref, dv_ref):
        last = table_ref[0] - 1
        dk_ref[...] = jnp.zeros_like(dk_ref)
        dv_ref[...] = jnp.zeros_like(dv_ref)
        t_ref[...] = jnp.zeros_like(t_ref)

        @pl.when(pl.program_id(0) == 0)
        def _():
            in_ref[...] = jnp.zeros_like(in_ref)

        def per_query(i, nothing):
            here = pl.ds(pl.multiple_of(i * BQ, BQ), BQ)
            start = start_ref[:, here]
            query = i * BQ + lax.broadcasted_iota(jnp.int32, (1, BQ), 1)
            cos, sin = cos_ref[here, :], sin_ref[here, :]

            def back(values):
                return values * cos - pltpu.roll(values, HEAD // 2, 1) * sin

            fixed_parts = []
            for h, c in enumerate(columns):
                g = g_ref[here, c]
                pairs = g.astype(F32) * att_ref[here, c].astype(F32)
                delta = jnp.sum(jnp.transpose(pairs), axis=0, keepdims=True)
                fixed_parts.append((q_ref[here, c], g, lse_ref[h, :, here], delta))

            def step(j, carry):
                at = pl.multiple_of(j * BK, BK)
                there = pl.ds(at, BK)
                key = at + lax.broadcasted_iota(jnp.int32, (BK, BQ), 0)
                seen = visible(start, query, key, last)
                results = []
                for c, (q, g, total, delta), dq in zip(columns, fixed_parts, carry):
                    k, v = k_ref[there, c], v_ref[there, c]
                    scores = dot(k, q, NT) * factor
                    weights = jnp.exp(jnp.where(seen, scores - total, MASKED))
                    slopes = (weights * (dot(v, g, NT) - delta)).astype(BF16)
                    dv_ref[there, c] += dot(weights.astype(BF16), g)
                    dk_ref[there, c] += dot(slopes, q)
                    results.append(dq + dot(slopes, k, TN))
                return tuple(results)

            empty = (jnp.zeros((BQ, HEAD), F32),) * together
            grads = lax.fori_loop(table_ref[1 + i], i + 1, step, empty)
            for h, c in enumerate(columns):
                gy = back(grads[h] * factor)
                both = gy * back(fixed_parts[h][0].astype(F32))
                t_ref[0, :, c] += jnp.sum(both, axis=0, keepdims=True)
                in_ref[here, :] += both
                out_ref[0, here, c] = (gy * s_ref[0, :, c]).astype(BF16)
            return nothing

        lax.fori_loop(0, blocks, per_query, 0)

        def per_key(i, nothing):
            here = pl.ds(pl.multiple_of(i * BQ, BQ), BQ)
            cos, sin = cos_ref[here, :], sin_ref[here, :]

            def back(values):
                return values * cos - pltpu.roll(values, HEAD // 2, 1) * sin

            for c in columns:
                gy = back(dk_ref[here, c] * factor)
                both = gy * back(k_ref[here, c].astype(F32))
                t_ref[1, :, c] += jnp.sum(both, axis=0, keepdims=True)
                out_ref[1, here, c] = (gy * s_ref[1, :, c]).astype(BF16)
                gv = dv_ref[here, c]
                more = gv * v_ref[here, c].astype(F32)
                t_ref[2, :, c] += jnp.sum(more, axis=0, keepdims=True)
                out_ref[2, here, c] = (gv * s_ref[2, :, c]).astype(BF16)
                in_ref[here, :] += both + more
            return nothing

        lax.fori_loop(0, blocks, per_key, 0)

    outs = (
        jax.ShapeDtypeStruct((3, length, local), BF16),
        jax.ShapeDtypeStruct((3, 1, local), F32),
        jax.ShapeDtypeStruct((length, HEAD), F32),
    )
    per_head = pl.BlockSpec((length, wide), lambda h, t: (0, h))
    return pl.pallas_call(
        body,
        out_shape=outs,
        grid_spec=pltpu.PrefetchScalarGridSpec(
            num_scalar_prefetch=1,
            grid=(steps,),
            in_specs=[
                per_head,
                pl.BlockSpec((length, wide), lambda h, t: (0, steps + h)),
                pl.BlockSpec((length, wide), lambda h, t: (0, 2 * steps + h)),
                per_head,
                per_head,
                pl.BlockSpec((together, 1, length), lambda h, t: (h, 0, 0)),
                fixed(starts.shape),
                fixed(cosine.shape),
                fixed(sine.shape),
                pl.BlockSpec((3, 1, wide), lambda h, t: (0, 0, h)),
            ],
            out_specs=[
                pl.BlockSpec((3, length, wide), lambda h, t: (0, 0, h)),
                pl.BlockSpec((3, 1, wide), lambda h, t: (0, 0, h)),
                pl.BlockSpec((length, HEAD), lambda h, t: (0, 0)),
            ],
            scratch_shapes=[pltpu.VMEM((length, wide), F32), pltpu.VMEM((length, wide), F32)],
        ),
        compiler_params=params(1),
        cost_estimate=cost(
            5 * length * length * local, bytes_of([qkv, grad, *outs]), length * length * heads // 2
        ),
        name="attention_backward",
    )(table, qkv, qkv, qkv, grad, attended, lse, starts, cosine, sine, scale)


def layer(
    n_dp,
    n_mp,
    tokens,
    norm_gains,
    query_key_value_weight,
    output_weight,
    gate_up_weight,
    down_weight,
    a_in,
    a_down,
    b_dmodel,
    b_hidden,
    m_dmodel,
    m_hidden,
    segment_ids,
    valid_mask,
    cotangent,
):
    length = segment_ids.shape[1]
    block = D // n_mp
    width = 2 * block
    hidden = FF // n_mp
    n_hi = n_mp // 4
    positions = 2 * n_hi
    chunk = length // CHUNKS
    me = lax.axis_index("mp")
    row = (me // ROW) % 2
    high_masks = [4 << k for k in range(n_hi.bit_length() - 1)]
    masks = [
        (high << 2) | (side << 1) | low
        for low in range(2)
        for high in range(n_hi)
        for side in range(2)
    ]
    parity = lax.axis_index("dp") % 2
    perm = jnp.concatenate([me ^ jnp.array(masks, jnp.int32), parity.astype(jnp.int32)[None]])

    def swapped(blocks):
        for k in range(n_mp.bit_length() - 1):
            bit = (me >> k) % 2 == 1
            blocks = [jnp.where(bit, blocks[i ^ (1 << k)], b) for i, b in enumerate(blocks)]
        return blocks

    def to_relative(values):
        blocks = swapped([values[:, i * block : (i + 1) * block] for i in range(n_mp)])
        return jnp.concatenate([blocks[k] for k in masks], axis=1)

    def flip(values, mask):
        return lax.ppermute(values, "mp", [(i, i ^ mask) for i in range(n_mp)])

    def gather(values):
        far = [values]
        for mask in high_masks:
            far = far + [flip(v, mask) for v in far]
        return far + [flip(f, 1) for f in far]

    def total(values):
        for mask in [1, *high_masks]:
            values = values + flip(values, mask)
        return values

    def total_relative(values):
        lead = values.shape[:-1]
        for mask in [1, *high_masks]:
            bit = n_hi if mask == 1 else mask >> 2
            cut = (*lead, positions // (2 * bit), 2, bit * width)
            theirs = flip(values, mask).reshape(cut)
            theirs = jnp.concatenate([theirs[..., 1:2, :], theirs[..., 0:1, :]], axis=-2)
            values = (values.reshape(cut) + theirs).reshape(values.shape)
        return values

    def reduce_far(near, far):
        blocks = [near, *far]
        for mask in reversed(high_masks):
            half = len(blocks) // 2
            sent = [flip(b.astype(BF16), mask) for b in blocks[half:]]
            blocks = [a.astype(F32) + b.astype(F32) for a, b in zip(blocks[:half], sent)]
        return blocks[0]

    def tie(*values):
        return lax.optimization_barrier(values)

    def scatter_begin(left, right, dims, *early):
        [odd] = matmul(left, right, dims, 1, width)
        theirs, *early = tie(flip(odd, 1), *early)
        outs = matmul(left, right, dims, 0, width, theirs)
        return (*outs, *early)

    def scatter_end(near, far=None):
        return reduce_far(near, [far[:, k * width : (k + 1) * width] for k in range(n_hi - 1)])

    spread_order = [("mp", 1)]
    spread_order += [("mp", k) for k in range(2, n_mp.bit_length() - 1)]
    spread_order += [("dp", k) for k in range(n_dp.bit_length() - 1)]
    spread_order += [("mp", 0)]

    def spread_step(values, axis, k):
        mine, count = (me, n_mp) if axis == "mp" else (lax.axis_index("dp"), n_dp)
        theirs = lax.ppermute(values, axis, [(i, i ^ (1 << k)) for i in range(count)])
        upper = (mine >> k) % 2 == 1
        return jnp.stack([jnp.where(upper, theirs, values), jnp.where(upper, values, theirs)])

    def spread_rest(values):
        shape = values.shape[1:]
        for axis, k in spread_order[1:]:
            values = spread_step(values, axis, k)
        added = spread_order[::-1]
        wanted = [("dp", k) for k in reversed(range(n_dp.bit_length() - 1))]
        wanted += [("mp", k) for k in reversed(range(n_mp.bit_length() - 1))]
        rank = len(added)
        values = jnp.transpose(values, (*[added.index(w) for w in wanted], rank, rank + 1))
        return values.reshape(n_dp * n_mp, *shape)

    def rows_of(values, which, c):
        return lax.dynamic_slice_in_dim(values, which * length + c * chunk, chunk, 0)

    def to_row(values):
        return [
            jnp.concatenate(
                [rows_of(values, row, c), flip(rows_of(values, 1 - row, c), ROW)], axis=1
            )
            for c in range(CHUNKS)
        ]

    def fetch(values, axis, parts=1, along=1):
        size = values.shape[axis] // 2
        half = lax.dynamic_slice_in_dim(values, parity * size, size, axis)
        same = [flip(v, ROW) for v in jnp.split(half, parts, axis=along)]
        rest = [lax.ppermute(v, "dp", [(i, i ^ 1) for i in range(n_dp)]) for v in same]
        return same, rest

    def from_row(chunks):
        theirs = jnp.concatenate([flip(v[:, block:], ROW) for v in chunks])
        mine = jnp.concatenate([v[:, :block] for v in chunks])
        return jnp.where(
            row == 0,
            jnp.concatenate([mine, theirs], axis=0),
            jnp.concatenate([theirs, mine], axis=0),
        )

    def cut(values):
        return [values[c * chunk : (c + 1) * chunk] for c in range(CHUNKS)]

    thin = a_in.shape[1]
    packs = [
        jnp.concatenate(
            [
                jnp.transpose(a_in, (0, 2, 1)).reshape(6 * RANK, thin),
                jnp.pad(
                    jnp.concatenate([b_dmodel.reshape(5 * RANK, thin), m_dmodel]),
                    ((0, RANK - 5), (0, 0)),
                ),
            ],
            axis=1,
        ).astype(BF16),
        jnp.concatenate(
            [jnp.transpose(a_down), b_hidden.reshape(2 * RANK, -1), m_hidden], axis=0
        ).astype(BF16),
    ]
    packs = [spread_step(p, *spread_order[0]) for p in packs]
    stream_cut = to_row(tokens)
    packs[0], packs[1], stream_cut[-1], qkv_own = tie(
        *packs, stream_cut[-1], query_key_value_weight
    )
    packs = [spread_rest(p) for p in packs]
    x_parts = [gather(v) for v in stream_cut]
    qkv_pieces = fetch(qkv_own, 1, 2)
    qkv_pieces[0][0], cot_own, out_own = tie(qkv_pieces[0][0], cotangent, output_weight)
    cot_cut = to_row(cot_own)
    out_pieces = [[flip(out_own, ROW)]]
    cot_parts = [gather(v) for v in cot_cut]
    low_rows, others = packs[0][:, :, :thin], packs[0][:, :, thin:]
    model = jnp.concatenate([low_rows, others[:, : 5 * RANK + 5]], axis=1)
    model_rows = 11 * RANK + 5
    model = to_relative(jnp.transpose(model, (1, 0, 2)).reshape(model_rows, D))
    wide = jnp.transpose(packs[1], (1, 0, 2)).reshape(3 * RANK + 2, n_mp, hidden)
    wide = jnp.concatenate(
        [lax.dynamic_index_in_dim(wide, i, 1, False) for i in (me, me ^ ROW)], axis=1
    )

    segments = lax.dynamic_slice_in_dim(segment_ids, row, 1, 0)
    valid = lax.dynamic_slice_in_dim(valid_mask, row, 1, 0)
    starts = jnp.zeros_like(segments)
    for s in range(SEGMENTS):
        count = jnp.sum((segments == s).astype(jnp.int32))
        starts = starts + jnp.where(segments > s, count, 0)
    table = jnp.concatenate([jnp.sum(valid, axis=1), starts[0, ::BQ] // BK])
    index = jnp.arange(length, dtype=jnp.int32)[None, :]
    frequency = ROPE_BASE ** (-(jnp.arange(HEAD // 2, dtype=F32) * (2.0 / HEAD)))
    angles = (index - starts)[0].astype(F32)[:, None] * frequency
    cos, sin = jnp.cos(angles), jnp.sin(angles)
    cosine = jnp.concatenate([cos, cos], axis=1)
    sine = jnp.concatenate([-sin, sin], axis=1)

    low_a = jnp.transpose(model[: 6 * RANK])
    model_b = [model[(6 + k) * RANK : (7 + k) * RANK] for k in range(5)]
    model_m = model[11 * RANK :].astype(F32)
    down_a = jnp.transpose(wide[:RANK])
    hidden_b = wide[RANK : 3 * RANK].reshape(2, RANK, 2 * hidden)
    hidden_m = wide[3 * RANK :].astype(F32)
    gains = to_relative(norm_gains)
    gain_columns = [gains[k].reshape(D, 1) for k in range(2)]
    lane = ((0, 0), (0, 128 - 6 * RANK))
    low_in = [jnp.pad((low_a.astype(F32) * g).astype(BF16), lane) for g in gain_columns]
    qkv_b = jnp.stack([b[:, :width] for b in model_b[:3]])
    qkv_v, qkv_sq = merge_columns(
        perm, query_key_value_weight, qkv_pieces, low_a, qkv_b, gain_columns[0], 0
    )
    gate_up_rows = jnp.transpose(gate_up_weight, (0, 2, 1))
    qkv_v, gate_up_own = tie(qkv_v, gate_up_rows)
    gate_up_pieces = fetch(gate_up_own, 0, 2)
    qkv_m = model_m[:3, :width].reshape(3, 1, width)
    qkv_scale = qkv_m * lax.rsqrt(qkv_sq)
    out_a = low_a[:width, 3 * RANK : 4 * RANK]
    out_v, out_sq = merge_rows(
        perm, output_weight[None], out_pieces, out_a[None], model_b[3][None]
    )
    qkv, qkv_u, r1, attended, lse = [], [], [], [], []
    keys, values = [], []
    cos_cut, sin_cut = cut(cosine), cut(sine)
    for c in range(CHUNKS):
        o, u, r = project_qkv(x_parts[c], qkv_v, low_in[0], qkv_scale, cos_cut[c], sin_cut[c])
        qkv.append(o)
        qkv_u.append(u)
        r1.append(r)
        keys.append(o[:, width : 2 * width])
        values.append(o[:, 2 * width :])
        query, cot_parts[c] = tie(o, cot_parts[c])
        att, l = attention_forward(
            table, query, jnp.concatenate(keys), jnp.concatenate(values), starts, c * chunk
        )
        attended.append(att)
        lse.append(l)
        if c == 0:
            qkv[0], down_own = tie(qkv[0], down_weight)
            down_pieces = fetch(down_own, 0)
    gu_v, gu_sq = merge_rows(
        perm,
        gate_up_rows,
        gate_up_pieces,
        jnp.transpose(hidden_b, (0, 2, 1)),
        model[4 * RANK : 6 * RANK].reshape(2, RANK, D),
        gains[1:2],
    )
    gu_sq = gu_sq.reshape(2, 1, 2 * hidden)
    gu_m = hidden_m.reshape(2, 1, 2 * hidden)
    gu_scale = gu_m * lax.rsqrt(gu_sq)
    down_v, down_sq = merge_rows(
        perm, down_weight[None], down_pieces, down_a[None], model_b[4][None]
    )
    out_sq = total_relative(out_sq[0])
    row_sq = jnp.concatenate([out_sq, total_relative(down_sq[0])], axis=0)
    row_m = model_m[3:5]
    out_scale = row_m[0:1] * lax.rsqrt(out_sq)
    down_scale = row_m[1:2] * lax.rsqrt(row_sq[1:2])
    out_rows, down_rows = out_v[0], down_v[0]

    middle, out_y, h_parts = [], [], []
    for c in range(CHUNKS):
        outs = scatter_begin(attended[c][None], out_v, NN, out_scale)
        out_scale = outs[-1]
        y = scatter_end(*outs[:-1]) * out_scale[:, :width]
        out_y.append(y)
        h = stream_cut[c].astype(F32) + y
        middle.append(h)
        h_parts.append(gather(h.astype(BF16)))
    hid, gu_u, down_u, r2 = [], [], [], []
    g_hidden, gu_t, down_gu = [], [], []
    grad_middle, grad_out_parts = [], []
    down_a_wide = jnp.pad(down_a, ((0, 0), (0, 128 - RANK)))
    down_b_wide = jnp.pad(model_b[4], ((0, 128 - RANK), (0, 0)))
    begun = []
    for c in range(CHUNKS):
        gate, up, h, ug, ud, r = project_hidden(
            h_parts[c], gu_v, low_in[1], gu_scale, down_a_wide
        )
        g, t, inner, low = hidden_backward(
            cot_parts[c], down_rows, down_scale, down_b_wide, gate, up, gu_scale
        )
        outs = scatter_begin(g, gu_v, NN, total(inner[:, 0]))
        if c + 1 < CHUNKS:
            h_parts[c + 1][0], near = tie(h_parts[c + 1][0], outs[0])
            outs = (near, *outs[1:])
        begun.append(outs)
        bags = (hid, gu_u, down_u, r2, g_hidden, gu_t, down_gu)
        for bag, value in zip(bags, (h, ug, ud, r, g, t, low)):
            bag.append(value)
    for c in range(CHUNKS):
        *outs, sums = begun[c]
        r = r2[c][:, :1]
        g = cot_cut[c].astype(F32) + r * scatter_end(*outs) - middle[c] * (r * r * (sums / D)[:, None])
        grad_middle.append(g)
        grad_out_parts.append(gather((g * out_scale[:, :width]).astype(BF16)))
    hid, g_hidden, _ = tie(hid, g_hidden, begun[-1][0])
    down_begun = [scatter_begin(hid[c][None], down_v, NN) for c in range(CHUNKS)]
    down_begun, grad_out_parts = tie(down_begun, grad_out_parts)
    grad_att = [matmul_parts(grad_out_parts[c], out_rows) for c in range(CHUNKS)]
    att_all = jnp.concatenate(attended)
    g_qkv, qkv_t, inner1 = attention_backward(
        table,
        jnp.concatenate(qkv),
        jnp.concatenate(grad_att),
        att_all,
        jnp.concatenate(lse, axis=2),
        starts,
        cosine,
        sine,
        qkv_scale,
    )
    down_y = [scatter_end(*outs) * down_scale[:, :width] for outs in down_begun]
    activations = [(middle[c] + down_y[c]).astype(BF16) for c in range(CHUNKS)]
    down_t = sum(jnp.sum(cot_cut[c].astype(F32) * down_y[c], axis=0) for c in range(CHUNKS))
    out_t = sum(jnp.sum(grad_middle[c] * out_y[c], axis=0) for c in range(CHUNKS))
    sums1 = total(jnp.sum(inner1, axis=1))
    begun = []
    for c in range(CHUNKS):
        outs = scatter_begin(g_qkv[:, c * chunk : (c + 1) * chunk], qkv_v, NT, sums1)
        sums1 = outs[-1]
        begun.append(outs[:-1])
    input_grad = []
    for c in range(CHUNKS):
        r = r1[c][:, :1]
        s = cut(sums1)[c][:, None]
        g = grad_middle[c] + r * scatter_end(*begun[c]) - stream_cut[c].astype(F32) * (r * r * (s / D))
        input_grad.append(g.astype(BF16))
    g_qkv, _ = tie(g_qkv, begun[-1][0])

    def over_tokens(left, right):
        return sum(dot(a, b, TN) for a, b in zip(left, right))

    def spread(lefts, parts):
        return jnp.concatenate(
            [over_tokens(lefts, [p[k] for p in parts]) for k in range(positions)], axis=1
        )

    def small(values):
        return values.astype(BF16)

    def halve(values, mask, axis):
        kept, sent = jnp.split(values, 2, axis=axis)
        return kept + flip(sent, mask)

    def to_block(values):
        values = halve(values, 1, 1)
        for mask in reversed(high_masks):
            values = halve(values, mask, 1)
        return values

    def to_owner(*arrays):
        mine = lax.axis_index("dp")
        here = [(d * n_mp + m, m * n_dp + d) for d in range(n_dp) for m in range(n_mp)]
        arrays = [halve(v, ROW, 1) for v in arrays]
        pieces = []
        for v in arrays:
            rows, size = v.shape
            pieces.append(jnp.transpose(v.reshape(rows, n_dp, size // n_dp), (1, 0, 2)))
        mask = n_dp // 2
        while mask:
            upper = (mine // mask) % 2 == 1
            for i, v in enumerate(pieces):
                low, high = v[:mask], v[mask:]
                sent = jnp.where(upper, low, high)
                sent = lax.ppermute(sent, "dp", [(i, i ^ mask) for i in range(n_dp)])
                pieces[i] = jnp.where(upper, high, low) + sent
            mask //= 2
        return [lax.ppermute(v[0], ("dp", "mp"), here) for v in pieces]

    gu_t = sum(gu_t)
    gu_coef = gu_t / gu_sq
    row_coef = jnp.concatenate(gather(jnp.stack([out_t, down_t])), axis=1) / row_sq
    out_coef, down_coef = row_coef[0:1], row_coef[1:2]
    gu_gu = []
    for c in range(CHUNKS):
        low = jnp.concatenate(
            [
                dot(g_hidden[c][0], hidden_b[0], NT),
                dot(g_hidden[c][1], hidden_b[1], NT),
            ],
            axis=1,
        )
        gu_gu.append(small(low * r2[c][:, :1]))
    gu_ga = 2.0 * gains[1:2] * spread(gu_gu, h_parts)
    gu_na = jnp.concatenate(
        [dot(small(hidden_b[k] * gu_coef[k]), gu_v[k]) for k in range(2)], axis=0
    )
    gu_ga = gu_ga - 2.0 / gains[1:2] * gu_na
    low_back = [small(model[: 6 * RANK].astype(F32) / gains[k : k + 1]) for k in range(2)]
    gu_gb = []
    for k in range(2):
        at = (4 + k) * RANK
        first = over_tokens([u[:, at : at + RANK] for u in gu_u], [g[k] for g in g_hidden])
        second = dot(low_back[1][at : at + RANK], gu_v[k], NT) * gu_coef[k]
        gu_gb.append(2.0 * (first - second))
    down_ga = over_tokens(down_gu, hid)[:RANK] - dot(
        small(model_b[4] * down_coef), down_rows, NT
    )
    down_gb = spread(down_u, cot_parts)[:RANK] * down_scale - dot(down_a, down_rows, TN) * down_coef
    qkv_coef = qkv_t / qkv_sq
    low = jnp.concatenate([dot(g_qkv[k], qkv_b[k], NT) for k in range(3)], axis=1)
    r1_all = jnp.concatenate(r1)[:, :1]
    qkv_gu = cut(small(low * r1_all))
    qkv_ga = 2.0 * gains[0:1] * spread(qkv_gu, x_parts)
    qkv_na = jnp.concatenate(
        [dot(small(qkv_b[k] * qkv_coef[k]), qkv_v[k], NT) for k in range(3)], axis=0
    )
    qkv_ga = qkv_ga - 2.0 / gains[0:1] * qkv_na
    u_all = jnp.concatenate(qkv_u)
    qkv_gb = []
    for k in range(3):
        at = k * RANK
        first = dot(u_all[:, at : at + RANK], g_qkv[k], TN)
        second = dot(low_back[0][at : at + RANK], qkv_v[k]) * qkv_coef[k]
        qkv_gb.append(2.0 * (first - second))
    out_gu, out_u = [], []
    for c in range(CHUNKS):
        out_gu.append(
            small(
                sum(
                    dot(grad_out_parts[c][p], model_b[3][:, p * width : (p + 1) * width], NT)
                    for p in range(positions)
                )
            )
        )
        out_u.append(small(dot(attended[c], out_a)))
    out_ga = over_tokens(out_gu, attended) - dot(small(model_b[3] * out_coef), out_rows, NT)
    out_gb = spread(out_u, grad_out_parts) - dot(out_a, out_rows, TN) * out_coef
    both = to_block(jnp.concatenate([qkv_ga, 2.0 * out_gb, gu_ga, 2.0 * down_gb]))
    model_grads, wide_grads = to_owner(
        jnp.concatenate(
            [
                both,
                2.0 * out_ga,
                *qkv_gb,
                (qkv_t / qkv_m).reshape(3, width),
                (out_t / row_m[0, :width])[None],
                (down_t / row_m[1, :width])[None],
            ]
        ),
        jnp.concatenate([2.0 * down_ga, *gu_gb, (gu_t / gu_m).reshape(2, 2 * hidden)]),
    )

    def stacked(values, count):
        return values.reshape(count, RANK, values.shape[1])

    def ranks(first, count):
        return stacked(model_grads[first * RANK : (first + count) * RANK], count)

    return (
        from_row(activations),
        from_row(input_grad),
        jnp.transpose(jnp.concatenate([ranks(0, 3), ranks(7, 1), ranks(4, 2)]), (0, 2, 1)),
        jnp.transpose(wide_grads[:RANK]),
        jnp.concatenate([ranks(8, 3), ranks(3, 1), ranks(6, 1)]),
        stacked(wide_grads[RANK : 3 * RANK], 2),
        model_grads[11 * RANK :],
        wide_grads[3 * RANK :],
    )


def solution(mesh):
    in_specs = (
        P("dp", "mp"),
        P(),
        P(None, None, "mp"),
        P("mp", None),
        P(None, None, "mp"),
        P("mp", None),
        P(None, ("dp", "mp"), None),
        P(("dp", "mp"), None),
        P(None, None, ("dp", "mp")),
        P(None, None, ("dp", "mp")),
        P(None, ("dp", "mp")),
        P(None, ("dp", "mp")),
        P("dp", None),
        P("dp", None),
        P("dp", "mp"),
    )
    out_specs = (
        P("dp", "mp"),
        P("dp", "mp"),
        P(None, ("dp", "mp"), None),
        P(("dp", "mp"), None),
        P(None, None, ("dp", "mp")),
        P(None, None, ("dp", "mp")),
        P(None, ("dp", "mp")),
        P(None, ("dp", "mp")),
    )
    local = functools.partial(layer, mesh.shape["dp"], mesh.shape["mp"])
    return jax.shard_map(local, mesh=mesh, in_specs=in_specs, out_specs=out_specs, check_vma=False)
```

```python
import functools

import jax
import jax.numpy as jnp
from jax import lax
from jax.experimental import pallas as pl
from jax.experimental.pallas import tpu as pltpu
from jax.sharding import PartitionSpec as P

D = 2048
HEAD = 128
FF = 5632
RANK = 16
SEGMENTS = 8
EPSILON = 1e-05
ROPE_BASE = 10000.0
MASKED = -1e30
ROW = 2
CHUNKS = 2
BQ = 256
BK = 256
HEADS_FORWARD = 2
HEADS_BACKWARD = 2
COST = 0.07
F32 = jnp.float32
BF16 = jnp.bfloat16

NN = (((1,), (0,)), ((), ()))
NT = (((1,), (1,)), ((), ()))
TN = (((0,), (0,)), ((), ()))


def dot(a, b, dims=NN):
    return lax.dot_general(a, b, dims, preferred_element_type=F32)


def params(rank):
    return pltpu.CompilerParams(
        dimension_semantics=("arbitrary",) * rank, vmem_limit_bytes=56 * 2**20
    )


def cost(flops, moved, exps=0):
    return pl.CostEstimate(
        flops=int(flops * COST), bytes_accessed=int(moved * COST), transcendentals=int(exps * COST)
    )


def bytes_of(arrays):
    return sum(a.size * a.dtype.itemsize for a in arrays)


def fixed(shape):
    rank = len(shape)
    return pl.BlockSpec(shape, lambda *_: (0,) * rank, pipeline_mode=pl.Buffered(1))


def tiles(width, step=768):
    return [(at, min(step, width - at)) for at in range(0, width, step)]


def merge_columns(perm, own, pieces, adapter_a, adapter_b, gain, first):
    count, rows, width = own.shape
    blocks = perm.shape[0] - 1
    size = rows // blocks
    local = adapter_b.shape[2]
    parts = 2 * len(pieces[0])
    deep = blocks // parts

    def body(perm_ref, own_ref, *rest):
        piece_refs = rest[:parts]
        a_ref, b_ref, gain_ref, v_ref, sq_ref = rest[parts:]
        at = perm_ref[pl.program_id(0)] // deep
        swap = perm_ref[blocks] * (parts // 2)
        place = jnp.where(at >= swap, at - swap, at + parts // 2)

        @pl.when(pl.program_id(0) == 0)
        def _():
            sq_ref[...] = jnp.zeros_like(sq_ref)

        for k in range(count):
            low = (first + k) * RANK
            product = dot(a_ref[:, low : low + RANK], b_ref[k])
            other = piece_refs[0][k].astype(F32)
            for i in range(1, parts):
                other = jnp.where(place == i, piece_refs[i][k].astype(F32), other)
            weight = jnp.concatenate([own_ref[k].astype(F32), other], axis=1)
            merged = weight + 2.0 * product
            sq_ref[k] += jnp.sum(merged * merged, axis=0, keepdims=True)
            v_ref[k] = (merged * gain_ref[...]).astype(BF16)

    return pl.pallas_call(
        body,
        out_shape=(
            jax.ShapeDtypeStruct((count, rows, local), BF16),
            jax.ShapeDtypeStruct((count, 1, local), F32),
        ),
        grid_spec=pltpu.PrefetchScalarGridSpec(
            num_scalar_prefetch=1,
            grid=(blocks,),
            in_specs=[
                pl.BlockSpec((count, size, width), lambda i, p: (0, p[i], 0)),
                *[pl.BlockSpec((count, size, width), lambda i, p: (0, p[i] % deep, 0))] * parts,
                pl.BlockSpec((size, adapter_a.shape[1]), lambda i, p: (i, 0)),
                fixed(adapter_b.shape),
                pl.BlockSpec((size, 1), lambda i, p: (i, 0)),
            ],
            out_specs=[
                pl.BlockSpec((count, size, local), lambda i, p: (0, i, 0)),
                pl.BlockSpec((count, 1, local), lambda i, p: (0, 0, 0)),
            ],
        ),
        compiler_params=params(1),
        cost_estimate=cost(4 * own.size * 64, 4 * bytes_of([own])),
        name="merge_columns",
    )(perm, own, *pieces[0], *pieces[1], adapter_a, adapter_b, gain)


def merge_rows(perm, own, pieces, adapter_a, adapter_b, gain=None):
    count, height, columns = own.shape
    blocks = perm.shape[0] - 1
    size = columns // blocks
    whole = len(pieces) == 1
    parts = len(pieces[0])
    pieces = [p.reshape(-1, columns) for group in pieces for p in group]
    tall = pieces[0].shape[0]

    def body(perm_ref, own_ref, *rest):
        piece_refs = rest[: len(pieces)]
        a_ref, b_ref, *extra = rest[len(pieces) :]
        v_ref, sq_ref = extra[-2:]
        held = [ref[...].astype(F32) for ref in piece_refs]
        if not whole:
            first = perm_ref[blocks] == 0
            low, high = held[:parts], held[parts:]
            found = [
                [jnp.where(first, a, b) for a, b in zip(low, high)],
                [jnp.where(first, b, a) for a, b in zip(low, high)],
            ]
        if gain is not None:

            @pl.when(pl.program_id(0) == 0)
            def _():
                sq_ref[...] = jnp.zeros_like(sq_ref)

        for k in range(count):
            product = dot(a_ref[k], b_ref[k])
            if whole:
                others = held
            else:
                others = [*found[0], *found[1]] if count == 1 else found[k]
            places = [(0, own_ref[k].astype(F32))]
            for i, other in enumerate(others):
                places.append((height + i * tall, other))
            down = None
            for at, weight in places:
                part = slice(at, at + weight.shape[0])
                merged = weight + 2.0 * product[part]
                square = merged * merged
                if gain is None:
                    more = jnp.sum(square, axis=0, keepdims=True)
                    down = more if down is None else down + more
                else:
                    sq_ref[k, part] += jnp.sum(square, axis=1, keepdims=True)
                    merged = merged * extra[0][...]
                v_ref[k, part] = merged.astype(BF16)
            if gain is None:
                sq_ref[k] = down

    if gain is None:
        squares = jax.ShapeDtypeStruct((count, 1, columns), F32)
        squares_spec = pl.BlockSpec((count, 1, size), lambda i, p: (0, 0, i))
        extra_specs, extra = [], []
    else:
        squares = jax.ShapeDtypeStruct((count, 2 * height, 1), F32)
        squares_spec = pl.BlockSpec((count, 2 * height, 1), lambda i, p: (0, 0, 0))
        extra_specs, extra = [pl.BlockSpec((1, size), lambda i, p: (0, i))], [gain]
    return pl.pallas_call(
        body,
        out_shape=(jax.ShapeDtypeStruct((count, 2 * height, columns), BF16), squares),
        grid_spec=pltpu.PrefetchScalarGridSpec(
            num_scalar_prefetch=1,
            grid=(blocks,),
            in_specs=[
                pl.BlockSpec((count, height, size), lambda i, p: (0, 0, p[i])),
                *[pl.BlockSpec((tall, size), lambda i, p: (0, p[i]))] * len(pieces),
                fixed(adapter_a.shape),
                pl.BlockSpec((count, RANK, size), lambda i, p: (0, 0, i)),
                *extra_specs,
            ],
            out_specs=[
                pl.BlockSpec((count, 2 * height, size), lambda i, p: (0, 0, i)),
                squares_spec,
            ],
        ),
        compiler_params=params(1),
        cost_estimate=cost(4 * own.size * 64, 4 * bytes_of([own])),
        name="merge_rows",
    )(perm, own, *pieces, adapter_a, adapter_b, *extra)


def inverse_rms(x):
    wide = x.astype(F32)
    return lax.rsqrt(jnp.sum(wide * wide, axis=1, keepdims=True) / D + EPSILON)


def project_qkv(parts, weights, low, scale, cosine, sine):
    rows, width = parts[0].shape
    local = weights.shape[2]
    bm = min(512, rows)

    def body(*refs):
        part_refs = refs[: len(parts)]
        v_ref, a_ref, s_ref, cos_ref, sin_ref, out_ref, u_ref, r_ref = refs[len(parts) :]
        x = jnp.concatenate([ref[...] for ref in part_refs], axis=1)
        r = inverse_rms(x)
        r_ref[...] = jnp.broadcast_to(r, r_ref.shape)
        u_ref[...] = (dot(x, a_ref[...]) * r).astype(BF16)
        cos, sin = cos_ref[...], sin_ref[...]
        for k in range(3):
            y = dot(x, v_ref[k]) * r * s_ref[k]
            for at in range(0, local, HEAD):
                head = y[:, at : at + HEAD]
                if k < 2:
                    head = head * cos + pltpu.roll(head, HEAD // 2, 1) * sin
                out_ref[:, k * local + at : k * local + at + HEAD] = head.astype(BF16)

    outs = (
        jax.ShapeDtypeStruct((rows, 3 * local), BF16),
        jax.ShapeDtypeStruct((rows, 128), BF16),
        jax.ShapeDtypeStruct((rows, 128), F32),
    )
    return pl.pallas_call(
        body,
        out_shape=outs,
        grid=(rows // bm,),
        in_specs=[pl.BlockSpec((bm, width), lambda i: (i, 0))] * len(parts)
        + [
            fixed(weights.shape),
            fixed(low.shape),
            fixed(scale.shape),
            pl.BlockSpec((bm, HEAD), lambda i: (i, 0)),
            pl.BlockSpec((bm, HEAD), lambda i: (i, 0)),
        ],
        out_specs=[
            pl.BlockSpec((bm, 3 * local), lambda i: (i, 0)),
            pl.BlockSpec((bm, 128), lambda i: (i, 0)),
            pl.BlockSpec((bm, 128), lambda i: (i, 0)),
        ],
        compiler_params=params(1),
        cost_estimate=cost(6 * rows * D * local, bytes_of([*parts, weights, *outs])),
        name="project_qkv",
    )(*parts, weights, low, scale, cosine, sine)


def project_hidden(parts, weights, low, scale, down_low):
    rows, width = parts[0].shape
    local = weights.shape[1]
    bm = min(512, rows)

    def body(*refs):
        part_refs = refs[: len(parts)]
        v_ref, a_ref, s_ref, d_ref, gate_ref, up_ref, hid_ref, u_ref, ud_ref, r_ref = refs[
            len(parts) :
        ]
        x = jnp.concatenate([ref[...] for ref in part_refs], axis=1)
        r = inverse_rms(x)
        r_ref[...] = jnp.broadcast_to(r, r_ref.shape)
        u_ref[...] = (dot(x, a_ref[...]) * r).astype(BF16)
        for at, size in tiles(local):
            cut = slice(at, at + size)
            gate = dot(x, v_ref[0, cut, :], NT) * r * s_ref[0, :, cut]
            up = dot(x, v_ref[1, cut, :], NT) * r * s_ref[1, :, cut]
            gate_ref[:, cut] = gate.astype(BF16)
            up_ref[:, cut] = up.astype(BF16)
            hid_ref[:, cut] = (gate * jax.nn.sigmoid(gate) * up).astype(BF16)
        ud_ref[...] = dot(hid_ref[...], d_ref[...]).astype(BF16)

    wide = jax.ShapeDtypeStruct((rows, local), BF16)
    outs = (
        wide,
        wide,
        wide,
        jax.ShapeDtypeStruct((rows, 128), BF16),
        jax.ShapeDtypeStruct((rows, 128), BF16),
        jax.ShapeDtypeStruct((rows, 128), F32),
    )
    return pl.pallas_call(
        body,
        out_shape=outs,
        grid=(rows // bm,),
        in_specs=[pl.BlockSpec((bm, width), lambda i: (i, 0))] * len(parts)
        + [fixed(weights.shape), fixed(low.shape), fixed(scale.shape), fixed(down_low.shape)],
        out_specs=[pl.BlockSpec((bm, local), lambda i: (i, 0))] * 3
        + [pl.BlockSpec((bm, 128), lambda i: (i, 0))] * 3,
        compiler_params=params(1),
        cost_estimate=cost(4 * rows * D * local, bytes_of([*parts, weights, *outs]), rows * local),
        name="project_hidden",
    )(*parts, weights, low, scale, down_low)


def hidden_backward(parts, down, down_scale, down_low, gate, up, scale):
    rows, width = parts[0].shape
    local = down.shape[0]
    bm = min(512, rows)

    def body(*refs):
        part_refs = refs[: len(parts)]
        v_ref, ds_ref, b_ref, gate_ref, up_ref, s_ref, out_ref, t_ref, in_ref, low_ref = refs[
            len(parts) :
        ]

        @pl.when(pl.program_id(0) == 0)
        def _():
            t_ref[...] = jnp.zeros_like(t_ref)

        raw = jnp.concatenate([ref[...] for ref in part_refs], axis=1).astype(F32)
        g = (raw * ds_ref[...]).astype(BF16)
        low_ref[...] = dot(g, b_ref[...], NT).astype(BF16)
        inner = jnp.zeros((bm, 1), F32)
        for at, size in tiles(local):
            cut = slice(at, at + size)
            back = dot(g, v_ref[cut, :], NT)
            y_gate = gate_ref[:, cut].astype(F32)
            y_up = up_ref[:, cut].astype(F32)
            sig = jax.nn.sigmoid(y_gate)
            act = y_gate * sig
            g_gate = back * y_up * (sig + act * (1.0 - sig))
            g_up = back * act
            dot_gate = g_gate * y_gate
            dot_up = g_up * y_up
            t_ref[0, :, cut] += jnp.sum(dot_gate, axis=0, keepdims=True)
            t_ref[1, :, cut] += jnp.sum(dot_up, axis=0, keepdims=True)
            inner += jnp.sum(dot_gate + dot_up, axis=1, keepdims=True)
            out_ref[0, :, cut] = (g_gate * s_ref[0, :, cut]).astype(BF16)
            out_ref[1, :, cut] = (g_up * s_ref[1, :, cut]).astype(BF16)
        in_ref[...] = jnp.broadcast_to(inner, in_ref.shape)

    outs = (
        jax.ShapeDtypeStruct((2, rows, local), BF16),
        jax.ShapeDtypeStruct((2, 1, local), F32),
        jax.ShapeDtypeStruct((rows, 128), F32),
        jax.ShapeDtypeStruct((rows, 128), BF16),
    )
    return pl.pallas_call(
        body,
        out_shape=outs,
        grid=(rows // bm,),
        in_specs=[pl.BlockSpec((bm, width), lambda i: (i, 0))] * len(parts)
        + [fixed(down.shape), fixed(down_scale.shape), fixed(down_low.shape)]
        + [pl.BlockSpec((bm, local), lambda i: (i, 0))] * 2
        + [fixed(scale.shape)],
        out_specs=[
            pl.BlockSpec((2, bm, local), lambda i: (0, i, 0)),
            pl.BlockSpec((2, 1, local), lambda i: (0, 0, 0)),
            pl.BlockSpec((bm, 128), lambda i: (i, 0)),
            pl.BlockSpec((bm, 128), lambda i: (i, 0)),
        ],
        compiler_params=params(1),
        cost_estimate=cost(
            2 * rows * D * local, bytes_of([*parts, down, gate, up, *outs]), rows * local
        ),
        name="hidden_backward",
    )(*parts, down, down_scale, down_low, gate, up, scale)


def matmul(left, right, dims, half, width, add=None):
    count, rows, depth = left.shape
    size = D // 2
    bm = rows if count > 1 else min(512, rows)
    split = [width, size - width] if add is not None else [size]
    split = [v for v in split if v]

    def body(left_ref, right_ref, *rest):
        outs = rest[-1 - len(split) : -1] if count > 1 else rest[-len(split) :]
        k = pl.program_id(1)
        total = dot(left_ref[...], right_ref[...], dims)
        if count > 1:
            acc_ref = rest[-1]

            @pl.when(k == 0)
            def _():
                acc_ref[...] = total

            @pl.when((k > 0) & (k < count - 1))
            def _():
                acc_ref[...] += total

        def finish():
            value = total + acc_ref[...] if count > 1 else total
            if add is not None:
                value = value + rest[0][...].astype(F32)
            at = 0
            for out, columns in zip(outs, split):
                out[...] = value[:, at : at + columns].astype(out.dtype)
                at += columns

        if count > 1:
            pl.when(k == count - 1)(finish)
        else:
            finish()

    specs = [pl.BlockSpec((None, bm, depth), lambda m, k: (k, m, 0))]
    if dims is NT:
        specs.append(pl.BlockSpec((None, size, depth), lambda m, k: (k, half, 0)))
    else:
        specs.append(pl.BlockSpec((None, depth, size), lambda m, k: (k, 0, half)))
    arrays = [left, right]
    if add is not None:
        specs.append(pl.BlockSpec((bm, size), lambda m, k: (m, 0)))
        arrays.append(add)
    kinds = [F32, BF16] if add is not None else [BF16]
    outs = [jax.ShapeDtypeStruct((rows, v), kind) for v, kind in zip(split, kinds)]
    return pl.pallas_call(
        body,
        out_shape=outs,
        grid=(rows // bm, count),
        in_specs=specs,
        out_specs=[pl.BlockSpec((bm, v), lambda m, k: (m, 0)) for v in split],
        scratch_shapes=[pltpu.VMEM((bm, size), F32)] if count > 1 else [],
        compiler_params=params(2),
        cost_estimate=cost(
            2 * count * rows * size * depth,
            bytes_of([left, *outs]) + 2 * count * size * depth,
        ),
        name="matmul_half",
    )(*arrays)


def matmul_parts(parts, right):
    rows, width = parts[0].shape
    out = jax.ShapeDtypeStruct((rows, right.shape[0]), BF16)
    bm = min(512, rows)

    def body(*refs):
        left = jnp.concatenate([ref[...] for ref in refs[: len(parts)]], axis=1)
        refs[-1][...] = dot(left, refs[-2][...], NT).astype(BF16)

    return pl.pallas_call(
        body,
        out_shape=out,
        grid=(rows // bm,),
        in_specs=[pl.BlockSpec((bm, width), lambda m: (m, 0))] * len(parts) + [fixed(right.shape)],
        out_specs=pl.BlockSpec((bm, right.shape[0]), lambda m: (m, 0)),
        compiler_params=params(1),
        cost_estimate=cost(2 * rows * D * right.shape[0], bytes_of([*parts, right, out])),
        name="matmul_parts",
    )(*parts, right)


def visible(start, query, key, last):
    return (key >= start) & ((key <= jnp.minimum(query, last)) | (key == query))


def attention_forward(table, qkv_q, keys, values, starts, offset):
    rows = qkv_q.shape[0]
    length, local = keys.shape
    heads = local // HEAD
    together = min(HEADS_FORWARD, heads)
    wide = together * HEAD
    factor = HEAD**-0.5

    def body(table_ref, q_ref, k_ref, v_ref, start_ref, out_ref, lse_ref):
        i = pl.program_id(1)
        base = offset + i * BQ
        start = start_ref[...]
        query = base + lax.broadcasted_iota(jnp.int32, (1, BQ), 1)
        last = table_ref[0] - 1
        columns = [slice(h * HEAD, (h + 1) * HEAD) for h in range(together)]
        queries = [q_ref[:, c] for c in columns]

        def step(j, carry):
            at = pl.multiple_of(j * BK, BK)
            key = at + lax.broadcasted_iota(jnp.int32, (BK, BQ), 0)
            seen = visible(start, query, key, last)
            results = []
            for c, q, (top, total, acc) in zip(columns, queries, carry):
                scores = dot(k_ref[pl.ds(at, BK), c], q, NT) * factor
                scores = jnp.where(seen, scores, MASKED)
                higher = jnp.maximum(top, jnp.max(scores, axis=0, keepdims=True))
                fade = jnp.exp(top - higher)
                weights = jnp.exp(scores - higher)
                total = total * fade + jnp.sum(weights, axis=0, keepdims=True)
                acc = acc * fade + dot(v_ref[pl.ds(at, BK), c], weights.astype(BF16), TN)
                results.append((higher, total, acc))
            return tuple(results)

        empty = (
            jnp.full((1, BQ), MASKED, F32),
            jnp.zeros((1, BQ), F32),
            jnp.zeros((HEAD, BQ), F32),
        )
        block = offset // BQ + i
        carry = lax.fori_loop(table_ref[1 + block], block + 1, step, (empty,) * together)
        for h, (top, total, acc) in enumerate(carry):
            out_ref[:, columns[h]] = jnp.transpose(acc / total).astype(BF16)
            lse_ref[h] = top + jnp.log(total)

    outs = (
        jax.ShapeDtypeStruct((rows, local), BF16),
        jax.ShapeDtypeStruct((heads, 1, rows), F32),
    )
    first = offset // BQ
    return pl.pallas_call(
        body,
        out_shape=outs,
        grid_spec=pltpu.PrefetchScalarGridSpec(
            num_scalar_prefetch=1,
            grid=(heads // together, rows // BQ),
            in_specs=[
                pl.BlockSpec((BQ, wide), lambda h, i, t: (i, h)),
                pl.BlockSpec((length, wide), lambda h, i, t: (0, h)),
                pl.BlockSpec((length, wide), lambda h, i, t: (0, h)),
                pl.BlockSpec((1, BQ), lambda h, i, t: (0, first + i)),
            ],
            out_specs=[
                pl.BlockSpec((BQ, wide), lambda h, i, t: (i, h)),
                pl.BlockSpec((together, 1, BQ), lambda h, i, t: (h, 0, i)),
            ],
        ),
        compiler_params=params(2),
        cost_estimate=cost(
            2 * rows * length * local, bytes_of([keys, values, *outs]), rows * length * heads // 2
        ),
        name="attention_forward",
    )(table, qkv_q, keys, values, starts)


def attention_backward(table, qkv, grad, attended, lse, starts, cosine, sine, scale):
    length = qkv.shape[0]
    local = grad.shape[1]
    heads = local // HEAD
    together = min(HEADS_BACKWARD, heads)
    wide = together * HEAD
    steps = heads // together
    factor = HEAD**-0.5
    blocks = length // BQ
    columns = [slice(h * HEAD, (h + 1) * HEAD) for h in range(together)]

    def body(table_ref, q_ref, k_ref, v_ref, g_ref, att_ref, lse_ref, start_ref, cos_ref, sin_ref, s_ref, out_ref, t_ref, in_ref, dk_ref, dv_ref):
        last = table_ref[0] - 1
        dk_ref[...] = jnp.zeros_like(dk_ref)
        dv_ref[...] = jnp.zeros_like(dv_ref)
        t_ref[...] = jnp.zeros_like(t_ref)

        @pl.when(pl.program_id(0) == 0)
        def _():
            in_ref[...] = jnp.zeros_like(in_ref)

        def per_query(i, nothing):
            here = pl.ds(pl.multiple_of(i * BQ, BQ), BQ)
            start = start_ref[:, here]
            query = i * BQ + lax.broadcasted_iota(jnp.int32, (1, BQ), 1)
            cos, sin = cos_ref[here, :], sin_ref[here, :]

            def back(values):
                return values * cos - pltpu.roll(values, HEAD // 2, 1) * sin

            fixed_parts = []
            for h, c in enumerate(columns):
                g = g_ref[here, c]
                pairs = g.astype(F32) * att_ref[here, c].astype(F32)
                delta = jnp.sum(jnp.transpose(pairs), axis=0, keepdims=True)
                fixed_parts.append((q_ref[here, c], g, lse_ref[h, :, here], delta))

            def step(j, carry):
                at = pl.multiple_of(j * BK, BK)
                there = pl.ds(at, BK)
                key = at + lax.broadcasted_iota(jnp.int32, (BK, BQ), 0)
                seen = visible(start, query, key, last)
                results = []
                for c, (q, g, total, delta), dq in zip(columns, fixed_parts, carry):
                    k, v = k_ref[there, c], v_ref[there, c]
                    scores = dot(k, q, NT) * factor
                    weights = jnp.exp(jnp.where(seen, scores - total, MASKED))
                    slopes = (weights * (dot(v, g, NT) - delta)).astype(BF16)
                    dv_ref[there, c] += dot(weights.astype(BF16), g)
                    dk_ref[there, c] += dot(slopes, q)
                    results.append(dq + dot(slopes, k, TN))
                return tuple(results)

            empty = (jnp.zeros((BQ, HEAD), F32),) * together
            grads = lax.fori_loop(table_ref[1 + i], i + 1, step, empty)
            for h, c in enumerate(columns):
                gy = back(grads[h] * factor)
                both = gy * back(fixed_parts[h][0].astype(F32))
                t_ref[0, :, c] += jnp.sum(both, axis=0, keepdims=True)
                in_ref[here, :] += both
                out_ref[0, here, c] = (gy * s_ref[0, :, c]).astype(BF16)
            return nothing

        lax.fori_loop(0, blocks, per_query, 0)

        def per_key(i, nothing):
            here = pl.ds(pl.multiple_of(i * BQ, BQ), BQ)
            cos, sin = cos_ref[here, :], sin_ref[here, :]

            def back(values):
                return values * cos - pltpu.roll(values, HEAD // 2, 1) * sin

            for c in columns:
                gy = back(dk_ref[here, c] * factor)
                both = gy * back(k_ref[here, c].astype(F32))
                t_ref[1, :, c] += jnp.sum(both, axis=0, keepdims=True)
                out_ref[1, here, c] = (gy * s_ref[1, :, c]).astype(BF16)
                gv = dv_ref[here, c]
                more = gv * v_ref[here, c].astype(F32)
                t_ref[2, :, c] += jnp.sum(more, axis=0, keepdims=True)
                out_ref[2, here, c] = (gv * s_ref[2, :, c]).astype(BF16)
                in_ref[here, :] += both + more
            return nothing

        lax.fori_loop(0, blocks, per_key, 0)

    outs = (
        jax.ShapeDtypeStruct((3, length, local), BF16),
        jax.ShapeDtypeStruct((3, 1, local), F32),
        jax.ShapeDtypeStruct((length, HEAD), F32),
    )
    per_head = pl.BlockSpec((length, wide), lambda h, t: (0, h))
    return pl.pallas_call(
        body,
        out_shape=outs,
        grid_spec=pltpu.PrefetchScalarGridSpec(
            num_scalar_prefetch=1,
            grid=(steps,),
            in_specs=[
                per_head,
                pl.BlockSpec((length, wide), lambda h, t: (0, steps + h)),
                pl.BlockSpec((length, wide), lambda h, t: (0, 2 * steps + h)),
                per_head,
                per_head,
                pl.BlockSpec((together, 1, length), lambda h, t: (h, 0, 0)),
                fixed(starts.shape),
                fixed(cosine.shape),
                fixed(sine.shape),
                pl.BlockSpec((3, 1, wide), lambda h, t: (0, 0, h)),
            ],
            out_specs=[
                pl.BlockSpec((3, length, wide), lambda h, t: (0, 0, h)),
                pl.BlockSpec((3, 1, wide), lambda h, t: (0, 0, h)),
                pl.BlockSpec((length, HEAD), lambda h, t: (0, 0)),
            ],
            scratch_shapes=[pltpu.VMEM((length, wide), F32), pltpu.VMEM((length, wide), F32)],
        ),
        compiler_params=params(1),
        cost_estimate=cost(
            5 * length * length * local, bytes_of([qkv, grad, *outs]), length * length * heads // 2
        ),
        name="attention_backward",
    )(table, qkv, qkv, qkv, grad, attended, lse, starts, cosine, sine, scale)


def layer(
    n_dp,
    n_mp,
    tokens,
    norm_gains,
    query_key_value_weight,
    output_weight,
    gate_up_weight,
    down_weight,
    a_in,
    a_down,
    b_dmodel,
    b_hidden,
    m_dmodel,
    m_hidden,
    segment_ids,
    valid_mask,
    cotangent,
):
    length = segment_ids.shape[1]
    block = D // n_mp
    width = 2 * block
    hidden = FF // n_mp
    n_hi = n_mp // 4
    positions = 2 * n_hi
    chunk = length // CHUNKS
    me = lax.axis_index("mp")
    row = (me // ROW) % 2
    high_masks = [4 << k for k in range(n_hi.bit_length() - 1)]
    masks = [
        (high << 2) | (side << 1) | low
        for low in range(2)
        for high in range(n_hi)
        for side in range(2)
    ]
    parity = lax.axis_index("dp") % 2
    perm = jnp.concatenate([me ^ jnp.array(masks, jnp.int32), parity.astype(jnp.int32)[None]])

    def swapped(blocks):
        for k in range(n_mp.bit_length() - 1):
            bit = (me >> k) % 2 == 1
            blocks = [jnp.where(bit, blocks[i ^ (1 << k)], b) for i, b in enumerate(blocks)]
        return blocks

    def to_relative(values):
        blocks = swapped([values[:, i * block : (i + 1) * block] for i in range(n_mp)])
        return jnp.concatenate([blocks[k] for k in masks], axis=1)

    def flip(values, mask):
        return lax.ppermute(values, "mp", [(i, i ^ mask) for i in range(n_mp)])

    def gather(values):
        far = [values]
        for mask in high_masks:
            far = far + [flip(v, mask) for v in far]
        return far + [flip(f, 1) for f in far]

    def total(values):
        for mask in [1, *high_masks]:
            values = values + flip(values, mask)
        return values

    def total_relative(values):
        lead = values.shape[:-1]
        for mask in [1, *high_masks]:
            bit = n_hi if mask == 1 else mask >> 2
            cut = (*lead, positions // (2 * bit), 2, bit * width)
            theirs = flip(values, mask).reshape(cut)
            theirs = jnp.concatenate([theirs[..., 1:2, :], theirs[..., 0:1, :]], axis=-2)
            values = (values.reshape(cut) + theirs).reshape(values.shape)
        return values

    def reduce_far(near, far):
        blocks = [near, *far]
        for mask in reversed(high_masks):
            half = len(blocks) // 2
            sent = [flip(b.astype(BF16), mask) for b in blocks[half:]]
            blocks = [a.astype(F32) + b.astype(F32) for a, b in zip(blocks[:half], sent)]
        return blocks[0]

    def tie(*values):
        return lax.optimization_barrier(values)

    def scatter_begin(left, right, dims, *early):
        [odd] = matmul(left, right, dims, 1, width)
        theirs, *early = tie(flip(odd, 1), *early)
        outs = matmul(left, right, dims, 0, width, theirs)
        return (*outs, *early)

    def scatter_end(near, far=None):
        return reduce_far(near, [far[:, k * width : (k + 1) * width] for k in range(n_hi - 1)])

    spread_order = [("mp", 1)]
    spread_order += [("mp", k) for k in range(2, n_mp.bit_length() - 1)]
    spread_order += [("dp", k) for k in range(n_dp.bit_length() - 1)]
    spread_order += [("mp", 0)]

    def spread_step(values, axis, k):
        mine, count = (me, n_mp) if axis == "mp" else (lax.axis_index("dp"), n_dp)
        theirs = lax.ppermute(values, axis, [(i, i ^ (1 << k)) for i in range(count)])
        upper = (mine >> k) % 2 == 1
        return jnp.stack([jnp.where(upper, theirs, values), jnp.where(upper, values, theirs)])

    def spread_rest(values):
        shape = values.shape[1:]
        for axis, k in spread_order[1:]:
            values = spread_step(values, axis, k)
        added = spread_order[::-1]
        wanted = [("dp", k) for k in reversed(range(n_dp.bit_length() - 1))]
        wanted += [("mp", k) for k in reversed(range(n_mp.bit_length() - 1))]
        rank = len(added)
        values = jnp.transpose(values, (*[added.index(w) for w in wanted], rank, rank + 1))
        return values.reshape(n_dp * n_mp, *shape)

    def rows_of(values, which, c):
        return lax.dynamic_slice_in_dim(values, which * length + c * chunk, chunk, 0)

    def to_row(values):
        return [
            jnp.concatenate(
                [rows_of(values, row, c), flip(rows_of(values, 1 - row, c), ROW)], axis=1
            )
            for c in range(CHUNKS)
        ]

    def fetch(values, axis, parts=1, along=1):
        size = values.shape[axis] // 2
        half = lax.dynamic_slice_in_dim(values, parity * size, size, axis)
        same = [flip(v, ROW) for v in jnp.split(half, parts, axis=along)]
        rest = [lax.ppermute(v, "dp", [(i, i ^ 1) for i in range(n_dp)]) for v in same]
        return same, rest

    def from_row(chunks):
        theirs = jnp.concatenate([flip(v[:, block:], ROW) for v in chunks])
        mine = jnp.concatenate([v[:, :block] for v in chunks])
        return jnp.where(
            row == 0,
            jnp.concatenate([mine, theirs], axis=0),
            jnp.concatenate([theirs, mine], axis=0),
        )

    def cut(values):
        return [values[c * chunk : (c + 1) * chunk] for c in range(CHUNKS)]

    thin = a_in.shape[1]
    packs = [
        jnp.concatenate(
            [
                jnp.transpose(a_in, (0, 2, 1)).reshape(6 * RANK, thin),
                jnp.pad(
                    jnp.concatenate([b_dmodel.reshape(5 * RANK, thin), m_dmodel]),
                    ((0, RANK - 5), (0, 0)),
                ),
            ],
            axis=1,
        ).astype(BF16),
        jnp.concatenate(
            [jnp.transpose(a_down), b_hidden.reshape(2 * RANK, -1), m_hidden], axis=0
        ).astype(BF16),
    ]
    packs = [spread_step(p, *spread_order[0]) for p in packs]
    stream_cut = to_row(tokens)
    packs[0], packs[1], stream_cut[-1], qkv_own = tie(
        *packs, stream_cut[-1], query_key_value_weight
    )
    packs = [spread_rest(p) for p in packs]
    x_parts = [gather(v) for v in stream_cut]
    qkv_pieces = fetch(qkv_own, 1, 2)
    qkv_pieces[0][0], cot_own, out_own = tie(qkv_pieces[0][0], cotangent, output_weight)
    cot_cut = to_row(cot_own)
    out_pieces = [[flip(out_own, ROW)]]
    cot_parts = [gather(v) for v in cot_cut]
    low_rows, others = packs[0][:, :, :thin], packs[0][:, :, thin:]
    model = jnp.concatenate([low_rows, others[:, : 5 * RANK + 5]], axis=1)
    model_rows = 11 * RANK + 5
    model = to_relative(jnp.transpose(model, (1, 0, 2)).reshape(model_rows, D))
    wide = jnp.transpose(packs[1], (1, 0, 2)).reshape(3 * RANK + 2, n_mp, hidden)
    wide = jnp.concatenate(
        [lax.dynamic_index_in_dim(wide, i, 1, False) for i in (me, me ^ ROW)], axis=1
    )

    segments = lax.dynamic_slice_in_dim(segment_ids, row, 1, 0)
    valid = lax.dynamic_slice_in_dim(valid_mask, row, 1, 0)
    starts = jnp.zeros_like(segments)
    for s in range(SEGMENTS):
        count = jnp.sum((segments == s).astype(jnp.int32))
        starts = starts + jnp.where(segments > s, count, 0)
    table = jnp.concatenate([jnp.sum(valid, axis=1), starts[0, ::BQ] // BK])
    index = jnp.arange(length, dtype=jnp.int32)[None, :]
    frequency = ROPE_BASE ** (-(jnp.arange(HEAD // 2, dtype=F32) * (2.0 / HEAD)))
    angles = (index - starts)[0].astype(F32)[:, None] * frequency
    cos, sin = jnp.cos(angles), jnp.sin(angles)
    cosine = jnp.concatenate([cos, cos], axis=1)
    sine = jnp.concatenate([-sin, sin], axis=1)

    low_a = jnp.transpose(model[: 6 * RANK])
    model_b = [model[(6 + k) * RANK : (7 + k) * RANK] for k in range(5)]
    model_m = model[11 * RANK :].astype(F32)
    down_a = jnp.transpose(wide[:RANK])
    hidden_b = wide[RANK : 3 * RANK].reshape(2, RANK, 2 * hidden)
    hidden_m = wide[3 * RANK :].astype(F32)
    gains = to_relative(norm_gains)
    gain_columns = [gains[k].reshape(D, 1) for k in range(2)]
    lane = ((0, 0), (0, 128 - 6 * RANK))
    low_in = [jnp.pad((low_a.astype(F32) * g).astype(BF16), lane) for g in gain_columns]
    qkv_b = jnp.stack([b[:, :width] for b in model_b[:3]])
    qkv_v, qkv_sq = merge_columns(
        perm, query_key_value_weight, qkv_pieces, low_a, qkv_b, gain_columns[0], 0
    )
    gate_up_rows = jnp.transpose(gate_up_weight, (0, 2, 1))
    qkv_v, gate_up_own = tie(qkv_v, gate_up_rows)
    gate_up_pieces = fetch(gate_up_own, 0, 2)
    qkv_m = model_m[:3, :width].reshape(3, 1, width)
    qkv_scale = qkv_m * lax.rsqrt(qkv_sq)
    out_a = low_a[:width, 3 * RANK : 4 * RANK]
    out_v, out_sq = merge_rows(
        perm, output_weight[None], out_pieces, out_a[None], model_b[3][None]
    )
    qkv, qkv_u, r1, attended, lse = [], [], [], [], []
    keys, values = [], []
    cos_cut, sin_cut = cut(cosine), cut(sine)
    for c in range(CHUNKS):
        o, u, r = project_qkv(x_parts[c], qkv_v, low_in[0], qkv_scale, cos_cut[c], sin_cut[c])
        qkv.append(o)
        qkv_u.append(u)
        r1.append(r)
        keys.append(o[:, width : 2 * width])
        values.append(o[:, 2 * width :])
        query, cot_parts[c] = tie(o, cot_parts[c])
        att, l = attention_forward(
            table, query, jnp.concatenate(keys), jnp.concatenate(values), starts, c * chunk
        )
        attended.append(att)
        lse.append(l)
        if c == 0:
            qkv[0], down_own = tie(qkv[0], down_weight)
            down_pieces = fetch(down_own, 0)
    gu_v, gu_sq = merge_rows(
        perm,
        gate_up_rows,
        gate_up_pieces,
        jnp.transpose(hidden_b, (0, 2, 1)),
        model[4 * RANK : 6 * RANK].reshape(2, RANK, D),
        gains[1:2],
    )
    gu_sq = gu_sq.reshape(2, 1, 2 * hidden)
    gu_m = hidden_m.reshape(2, 1, 2 * hidden)
    gu_scale = gu_m * lax.rsqrt(gu_sq)
    down_v, down_sq = merge_rows(
        perm, down_weight[None], down_pieces, down_a[None], model_b[4][None]
    )
    out_sq = total_relative(out_sq[0])
    row_sq = jnp.concatenate([out_sq, total_relative(down_sq[0])], axis=0)
    row_m = model_m[3:5]
    out_scale = row_m[0:1] * lax.rsqrt(out_sq)
    down_scale = row_m[1:2] * lax.rsqrt(row_sq[1:2])
    out_rows, down_rows = out_v[0], down_v[0]

    middle, out_y, h_parts = [], [], []
    for c in range(CHUNKS):
        outs = scatter_begin(attended[c][None], out_v, NN, out_scale)
        out_scale = outs[-1]
        y = scatter_end(*outs[:-1]) * out_scale[:, :width]
        out_y.append(y)
        h = stream_cut[c].astype(F32) + y
        middle.append(h)
        h_parts.append(gather(h.astype(BF16)))
    hid, gu_u, down_u, r2 = [], [], [], []
    g_hidden, gu_t, down_gu = [], [], []
    grad_middle, grad_out_parts = [], []
    down_a_wide = jnp.pad(down_a, ((0, 0), (0, 128 - RANK)))
    down_b_wide = jnp.pad(model_b[4], ((0, 128 - RANK), (0, 0)))
    begun = []
    for c in range(CHUNKS):
        gate, up, h, ug, ud, r = project_hidden(
            h_parts[c], gu_v, low_in[1], gu_scale, down_a_wide
        )
        g, t, inner, low = hidden_backward(
            cot_parts[c], down_rows, down_scale, down_b_wide, gate, up, gu_scale
        )
        outs = scatter_begin(g, gu_v, NN, total(inner[:, 0]))
        if c + 1 < CHUNKS:
            h_parts[c + 1][0], near = tie(h_parts[c + 1][0], outs[0])
            outs = (near, *outs[1:])
        begun.append(outs)
        bags = (hid, gu_u, down_u, r2, g_hidden, gu_t, down_gu)
        for bag, value in zip(bags, (h, ug, ud, r, g, t, low)):
            bag.append(value)
    for c in range(CHUNKS):
        *outs, sums = begun[c]
        r = r2[c][:, :1]
        g = cot_cut[c].astype(F32) + r * scatter_end(*outs) - middle[c] * (r * r * (sums / D)[:, None])
        grad_middle.append(g)
        grad_out_parts.append(gather((g * out_scale[:, :width]).astype(BF16)))
    hid, g_hidden, _ = tie(hid, g_hidden, begun[-1][0])
    down_begun = [scatter_begin(hid[c][None], down_v, NN) for c in range(CHUNKS)]
    down_begun, grad_out_parts = tie(down_begun, grad_out_parts)
    grad_att = [matmul_parts(grad_out_parts[c], out_rows) for c in range(CHUNKS)]
    att_all = jnp.concatenate(attended)
    g_qkv, qkv_t, inner1 = attention_backward(
        table,
        jnp.concatenate(qkv),
        jnp.concatenate(grad_att),
        att_all,
        jnp.concatenate(lse, axis=2),
        starts,
        cosine,
        sine,
        qkv_scale,
    )
    down_y = [scatter_end(*outs) * down_scale[:, :width] for outs in down_begun]
    activations = [(middle[c] + down_y[c]).astype(BF16) for c in range(CHUNKS)]
    down_t = sum(jnp.sum(cot_cut[c].astype(F32) * down_y[c], axis=0) for c in range(CHUNKS))
    out_t = sum(jnp.sum(grad_middle[c] * out_y[c], axis=0) for c in range(CHUNKS))
    sums1 = total(jnp.sum(inner1, axis=1))
    begun = []
    for c in range(CHUNKS):
        outs = scatter_begin(g_qkv[:, c * chunk : (c + 1) * chunk], qkv_v, NT, sums1)
        sums1 = outs[-1]
        begun.append(outs[:-1])
    input_grad = []
    for c in range(CHUNKS):
        r = r1[c][:, :1]
        s = cut(sums1)[c][:, None]
        g = grad_middle[c] + r * scatter_end(*begun[c]) - stream_cut[c].astype(F32) * (r * r * (s / D))
        input_grad.append(g.astype(BF16))
    g_qkv, _ = tie(g_qkv, begun[-1][0])

    def over_tokens(left, right):
        return sum(dot(a, b, TN) for a, b in zip(left, right))

    def spread(lefts, parts):
        return jnp.concatenate(
            [over_tokens(lefts, [p[k] for p in parts]) for k in range(positions)], axis=1
        )

    def small(values):
        return values.astype(BF16)

    def halve(values, mask, axis):
        kept, sent = jnp.split(values, 2, axis=axis)
        return kept + flip(sent, mask)

    def to_block(values):
        values = halve(values, 1, 1)
        for mask in reversed(high_masks):
            values = halve(values, mask, 1)
        return values

    def to_owner(*arrays):
        mine = lax.axis_index("dp")
        here = [(d * n_mp + m, m * n_dp + d) for d in range(n_dp) for m in range(n_mp)]
        arrays = [halve(v, ROW, 1) for v in arrays]
        pieces = []
        for v in arrays:
            rows, size = v.shape
            pieces.append(jnp.transpose(v.reshape(rows, n_dp, size // n_dp), (1, 0, 2)))
        mask = n_dp // 2
        while mask:
            upper = (mine // mask) % 2 == 1
            for i, v in enumerate(pieces):
                low, high = v[:mask], v[mask:]
                sent = jnp.where(upper, low, high)
                sent = lax.ppermute(sent, "dp", [(i, i ^ mask) for i in range(n_dp)])
                pieces[i] = jnp.where(upper, high, low) + sent
            mask //= 2
        return [lax.ppermute(v[0], ("dp", "mp"), here) for v in pieces]

    gu_t = sum(gu_t)
    gu_coef = gu_t / gu_sq
    row_coef = jnp.concatenate(gather(jnp.stack([out_t, down_t])), axis=1) / row_sq
    out_coef, down_coef = row_coef[0:1], row_coef[1:2]
    gu_gu = []
    for c in range(CHUNKS):
        low = jnp.concatenate(
            [
                dot(g_hidden[c][0], hidden_b[0], NT),
                dot(g_hidden[c][1], hidden_b[1], NT),
            ],
            axis=1,
        )
        gu_gu.append(small(low * r2[c][:, :1]))
    gu_ga = 2.0 * gains[1:2] * spread(gu_gu, h_parts)
    gu_na = jnp.concatenate(
        [dot(small(hidden_b[k] * gu_coef[k]), gu_v[k]) for k in range(2)], axis=0
    )
    gu_ga = gu_ga - 2.0 / gains[1:2] * gu_na
    low_back = [small(model[: 6 * RANK].astype(F32) / gains[k : k + 1]) for k in range(2)]
    gu_gb = []
    for k in range(2):
        at = (4 + k) * RANK
        first = over_tokens([u[:, at : at + RANK] for u in gu_u], [g[k] for g in g_hidden])
        second = dot(low_back[1][at : at + RANK], gu_v[k], NT) * gu_coef[k]
        gu_gb.append(2.0 * (first - second))
    down_ga = over_tokens(down_gu, hid)[:RANK] - dot(
        small(model_b[4] * down_coef), down_rows, NT
    )
    down_gb = spread(down_u, cot_parts)[:RANK] * down_scale - dot(down_a, down_rows, TN) * down_coef
    qkv_coef = qkv_t / qkv_sq
    low = jnp.concatenate([dot(g_qkv[k], qkv_b[k], NT) for k in range(3)], axis=1)
    r1_all = jnp.concatenate(r1)[:, :1]
    qkv_gu = cut(small(low * r1_all))
    qkv_ga = 2.0 * gains[0:1] * spread(qkv_gu, x_parts)
    qkv_na = jnp.concatenate(
        [dot(small(qkv_b[k] * qkv_coef[k]), qkv_v[k], NT) for k in range(3)], axis=0
    )
    qkv_ga = qkv_ga - 2.0 / gains[0:1] * qkv_na
    u_all = jnp.concatenate(qkv_u)
    qkv_gb = []
    for k in range(3):
        at = k * RANK
        first = dot(u_all[:, at : at + RANK], g_qkv[k], TN)
        second = dot(low_back[0][at : at + RANK], qkv_v[k]) * qkv_coef[k]
        qkv_gb.append(2.0 * (first - second))
    out_gu, out_u = [], []
    for c in range(CHUNKS):
        out_gu.append(
            small(
                sum(
                    dot(grad_out_parts[c][p], model_b[3][:, p * width : (p + 1) * width], NT)
                    for p in range(positions)
                )
            )
        )
        out_u.append(small(dot(attended[c], out_a)))
    out_ga = over_tokens(out_gu, attended) - dot(small(model_b[3] * out_coef), out_rows, NT)
    out_gb = spread(out_u, grad_out_parts) - dot(out_a, out_rows, TN) * out_coef
    both = to_block(jnp.concatenate([qkv_ga, 2.0 * out_gb, gu_ga, 2.0 * down_gb]))
    model_grads, wide_grads = to_owner(
        jnp.concatenate(
            [
                both,
                2.0 * out_ga,
                *qkv_gb,
                (qkv_t / qkv_m).reshape(3, width),
                (out_t / row_m[0, :width])[None],
                (down_t / row_m[1, :width])[None],
            ]
        ),
        jnp.concatenate([2.0 * down_ga, *gu_gb, (gu_t / gu_m).reshape(2, 2 * hidden)]),
    )

    def stacked(values, count):
        return values.reshape(count, RANK, values.shape[1])

    def ranks(first, count):
        return stacked(model_grads[first * RANK : (first + count) * RANK], count)

    return (
        from_row(activations),
        from_row(input_grad),
        jnp.transpose(jnp.concatenate([ranks(0, 3), ranks(7, 1), ranks(4, 2)]), (0, 2, 1)),
        jnp.transpose(wide_grads[:RANK]),
        jnp.concatenate([ranks(8, 3), ranks(3, 1), ranks(6, 1)]),
        stacked(wide_grads[RANK : 3 * RANK], 2),
        model_grads[11 * RANK :],
        wide_grads[3 * RANK :],
    )


def solution(mesh):
    in_specs = (
        P("dp", "mp"),
        P(),
        P(None, None, "mp"),
        P("mp", None),
        P(None, None, "mp"),
        P("mp", None),
        P(None, ("dp", "mp"), None),
        P(("dp", "mp"), None),
        P(None, None, ("dp", "mp")),
        P(None, None, ("dp", "mp")),
        P(None, ("dp", "mp")),
        P(None, ("dp", "mp")),
        P("dp", None),
        P("dp", None),
        P("dp", "mp"),
    )
    out_specs = (
        P("dp", "mp"),
        P("dp", "mp"),
        P(None, ("dp", "mp"), None),
        P(("dp", "mp"), None),
        P(None, None, ("dp", "mp")),
        P(None, None, ("dp", "mp")),
        P(None, ("dp", "mp")),
        P(None, ("dp", "mp")),
    )
    local = functools.partial(layer, mesh.shape["dp"], mesh.shape["mp"])
    return jax.shard_map(local, mesh=mesh, in_specs=in_specs, out_specs=out_specs, check_vma=False)
```
